32 devices in a mesh: walk: 8 (over y, x, core), par: 4 (over z).
Axes of the slice: x: 2, y: 2, z: 4, core: 2. Of those that a mesh axis runs over, the one named last changes fastest.
Arguments:
- features: bfloat16 [1536, 32, 256], P(('walk', 'par')), may hold values from -6 to 6
- signals: bfloat16 [1536, 32, 256], P(('walk', 'par')), may hold values from -6 to 6
- param_scale: float32 [256, 256], replicated, may hold values from 0.2 to 2
- geometry: int32 [1536], replicated, may hold values from 0 to 63
- electrons: int32 [64], replicated, may hold values from 16 to 32
Outputs:
- panel: float32 [1536, 256], P('walk')
- trailing: float32 [1536, 1536], P('walk', 'par')
The draws below stay inside these ranges and needn't reach their ends.
All inputs are finite; a program needn't handle non-finite values.
Results may differ from the reference program's by a relative error of at most 0.0003.
Values sent between devices are 32-bit elements; how exact they have to be, the bound alone decides.
No kernel may reach another device: no remote copies, remote signals or barrier semaphores. Data moves between devices by JAX's collectives and lax.ppermute only.
A program may use at most 256 MiB of HBM per device.

```python
import math
import jax
import jax.numpy as jnp
from jax import lax

D = 256
E = 32
G = 64
PB = 256
NW = 1536


def place_ends(result, own_key, low, largest):
    index_at = [jax.random.randint(jax.random.fold_in(own_key, axis), (), 0, length) for axis, length in enumerate(result.shape)]
    widest = result.shape.index(max(result.shape))
    next_to = index_at[:widest] + [(index_at[widest] + 1) % result.shape[widest]] + index_at[widest + 1:]
    return result.at[tuple(index_at)].set(low).at[tuple(next_to)].set(largest)


def level_of(key, shape, shards, low, largest):
    level, own = 1.0, jax.random.fold_in(key, 6)
    for position, shards_of in shards:
        steps = jnp.exp(jax.random.uniform(jax.random.fold_in(own, position), (shards_of,), jnp.float32, low / len(shards), largest / len(shards)))
        level = level * jnp.repeat(steps, shape[position] // shards_of).reshape([-1 if axis == position else 1 for axis in range(len(shape))])
    return level


def gaussian(stream_key, dims, width, most, shards=(), held_as=jnp.bfloat16):
    gain = level_of(stream_key, dims, shards, -0.22, 0.18) if shards else 1.0
    values = jax.random.normal(stream_key, dims, jnp.float32) * width * gain
    return jnp.minimum(jnp.maximum(values, -most), most).astype(held_as)


def setup_inputs(seed: int = 0) -> dict:
    key_list = jax.random.split(jax.random.key(seed), 6)
    features = gaussian(key_list[0], (NW, E, D), 1.0, 6.0, ((0, 32),))
    signals = gaussian(key_list[1], (NW, E, D), 1.0, 6.0, ((0, 32),))
    param_scale = jnp.clip(jnp.exp(jax.random.uniform(key_list[2], (D, D), jnp.float32, math.log(0.2), math.log(2.0))), 0.2, 2.0)
    geometry = place_ends(jax.random.randint(key_list[3], (NW,), 0, G), jax.random.fold_in(key_list[3], 1), 0, G - 1).astype(jnp.int32)
    electrons = place_ends(jax.random.randint(key_list[4], (G,), E // 2, E + 1), jax.random.fold_in(key_list[4], 1), E // 2, E).astype(jnp.int32)
    return {"features": features, "signals": signals, "param_scale": param_scale, "geometry": geometry, "electrons": electrons}


HIGHEST = lax.Precision.HIGHEST
SHIFT = 0.05

def reference(features, signals, param_scale, geometry, electrons):
    walkers = features.shape[0]
    group_ids = jnp.arange(G, dtype=jnp.int32)
    matches = geometry[:, None] == group_ids[None, :]
    onehot = matches.astype(jnp.float32)
    counts = jnp.maximum(lax.optimization_barrier(jnp.sum(onehot, axis=0)), 1.0)
    per_walker = lax.optimization_barrier(jnp.sum(jnp.where(matches, electrons[None, :], 0), axis=1))
    live = (jnp.arange(E, dtype=jnp.int32)[None, :] < per_walker[:, None]).astype(jnp.float32)
    left_side = features.astype(jnp.float32) * live[:, :, None]
    right_side = signals.astype(jnp.float32)
    norm_factor = 1.0 / math.sqrt(E * D * D)
    row_step = D // 8

    def accumulate(total, offset):
        portion = lax.dynamic_slice_in_dim(left_side, offset, row_step, 2)
        scales = lax.dynamic_slice_in_dim(param_scale, offset, row_step, 0)
        block_jac = jnp.einsum('wei,wej->wij', portion, right_side, precision=HIGHEST)
        block_jac = block_jac * scales[None] * norm_factor
        flat = block_jac.reshape(walkers, row_step * D)
        means = jnp.dot(onehot.T, flat, precision=HIGHEST) / counts[:, None]
        centred = flat - jnp.dot(onehot, means, precision=HIGHEST)
        return (total + jnp.dot(centred, centred.T, precision=HIGHEST), None)
    offsets = jnp.arange(8, dtype=jnp.int32) * row_step
    gram, _ = lax.scan(accumulate, jnp.zeros((walkers, walkers), jnp.float32), offsets)
    shifted = gram + SHIFT * jnp.eye(walkers, dtype=jnp.float32)
    factor_head = jnp.linalg.cholesky(shifted[:PB, :PB])
    head_inverse = jax.scipy.linalg.solve_triangular(factor_head, jnp.eye(PB, dtype=jnp.float32), lower=True)
    panel = jnp.dot(shifted[:, :PB], head_inverse.T, precision=HIGHEST)
    trailing = shifted - jnp.dot(panel, panel.T, precision=HIGHEST)
    return (panel, trailing)
```

```python
import functools
import math

import jax
import jax.numpy as jnp
import numpy as np
from jax import lax
from jax.experimental import pallas as pl
from jax.experimental.pallas import tpu as pltpu
from jax.sharding import PartitionSpec as P

PB = 256
HIGHEST = lax.Precision.HIGHEST
SHIFT = 0.05
LANES = 256
CONTRACT_LAST = (((1,), (1,)), ((), ()))
VMEM_LIMIT = 60 * 1024 * 1024


def outer_rows(left_rows, right_rows):
    return lax.dot_general(left_rows, right_rows, CONTRACT_LAST, precision=HIGHEST)


def xor_pairs(size, bit):
    return [(i, i ^ bit) for i in range(size)]


class Plan:
    def __init__(self, walk_size, par_size):
        self.walk_size, self.par_size = walk_size, par_size
        par_bits = par_size.bit_length() - 1
        walk_bits = walk_size.bit_length() - 1
        self.dims = []
        for bit in reversed(range(par_bits)):
            self.dims.append(("par", 1 << bit, "J" if bit == 0 else "I"))
        for bit in range(1, walk_bits):
            self.dims.append(("walk", 1 << bit, "J" if bit == walk_bits - 1 else "I"))
        self.place = []
        seen = {"I": 0, "J": 0}
        for _, _, kind in self.dims:
            self.place.append(seen[kind])
            seen[kind] += 1
        self.blocks = {"F": 1 << seen["I"], "S": 1 << seen["J"]}
        self.rounds = self.schedule()

    def splits(self, side, kind):
        return (side == "F") == (kind == "I")

    def depth(self, side, src, rb, first):
        best = 0
        for k in range(first, len(self.dims)):
            kind = self.dims[k][2]
            if self.splits(side, kind):
                if rb >> self.place[k] & 1:
                    return max(best, 1 + self.depth(side, src, rb ^ (1 << self.place[k]), k + 1))
            else:
                best = max(best, 1 + self.depth(side, src, rb, k + 1))
        return best

    def tasks(self):
        out = []
        for side in ("F", "S"):
            live = [(0, rb) for rb in range(self.blocks[side])]
            for k, (_, _, kind) in enumerate(self.dims):
                kept, made = [], []
                for src, rb in live:
                    if self.splits(side, kind):
                        p = self.place[k]
                        if rb >> p & 1:
                            made.append((k, (side, src, rb), (side, src | 1 << k, rb ^ (1 << p))))
                        else:
                            kept.append((src, rb))
                    else:
                        kept.append((src, rb))
                        made.append((k, (side, src, rb), (side, src | 1 << k, rb)))
                live = kept + [dst[1:] for _, _, dst in made]
                out += made
        return out

    def schedule(self):
        left = self.tasks()
        have = {(side, 0, rb) for side in ("F", "S") for rb in range(self.blocks[side])}
        rounds = []
        while left:
            chosen = []
            for k, (axis, _, _) in enumerate(self.dims):
                ready = [t for t in left if t[0] == k and t[1] in have]
                ready.sort(key=lambda t: -self.depth(t[2][0], t[2][1], t[2][2], k + 1))
                chosen += ready[: 1 if axis == "par" else 2]
            left = [t for t in left if t not in chosen]
            have |= {t[2] for t in chosen}
            rounds.append(chosen)
        return rounds

    def flip(self, src):
        walk = par = 0
        for k, (axis, bit, _) in enumerate(self.dims):
            if src >> k & 1:
                walk, par = (walk | bit, par) if axis == "walk" else (walk, par | bit)
        return walk, par


def permute(value, axis, size, bit):
    return lax.ppermute(value, axis, xor_pairs(size, bit))


def exchange(plan, pieces):
    sizes = {"walk": plan.walk_size, "par": plan.par_size}
    held = dict(pieces)
    stacks = {"F": [], "S": []}
    fresh = [("F", 0, 0), ("S", 0, 0)]
    gate = []
    for chosen in plan.rounds + [[]]:
        groups = {}
        for k, src, dst in chosen:
            groups.setdefault((k, held[src].shape), []).append((src, dst))
        stacked = {}
        for side in ("F", "S"):
            names = [n for n in fresh if n[0] == side]
            if names:
                stacked[side] = names
        keys = sorted({s for pairs in groups.values() for s, _ in pairs} | set(fresh))
        if gate:
            tied = lax.optimization_barrier(tuple(held[n] for n in keys) + tuple(held[n] for n in gate))
            for n, v in zip(keys + gate, tied):
                held[n] = v
        fresh, gate = [], []
        for (k, _), pairs in groups.items():
            axis, bit, _ = plan.dims[k]
            if len(pairs) == 1:
                held[pairs[0][1]] = permute(held[pairs[0][0]], axis, sizes[axis], bit)
            else:
                moved = permute(jnp.stack([held[s] for s, _ in pairs]), axis, sizes[axis], bit)
                for i, (_, d) in enumerate(pairs):
                    held[d] = moved[i]
            gate += [d for _, d in pairs]
            fresh += [d for _, d in pairs if d[2] == 0]
        for side, names in stacked.items():
            own = jnp.stack([held[n] for n in names])
            other = permute(own, "walk", plan.walk_size, 1)
            stacks[side].append(([(n[1], 0) for n in names], own))
            stacks[side].append(([(n[1], 1) for n in names], other))
    return stacks


def gathered(stacks, order):
    sources = [s for names, _ in stacks for s in names]
    whole = jnp.concatenate([a for _, a in stacks], axis=0)
    return whole, sources


def jacobian_kernel(slots, rows_ref, f_ref, s_ref, scale_ref, out_ref):
    del rows_ref
    ib, lanes = f_ref.shape[1:]
    jb = s_ref.shape[1]
    together = LANES // slots
    parts = LANES // jb
    tiles = ib // parts
    lane = lax.broadcasted_iota(jnp.int32, (together, LANES), 1)
    row = lax.broadcasted_iota(jnp.int32, (together, LANES), 0)
    mine = (lane >= row * slots) & (lane < row * slots + slots)
    for g in range(lanes // LANES):
        left = f_ref[0, :, g * LANES : (g + 1) * LANES]
        right = s_ref[0, :, g * LANES : (g + 1) * LANES].astype(jnp.bfloat16)
        spread = jnp.where(mine[None], left[:, None, :], 0.0).reshape(ib * together, LANES)
        block = lax.dot_general(
            spread.astype(jnp.bfloat16), right, CONTRACT_LAST, preferred_element_type=jnp.float32
        )
        block = block.reshape(parts, tiles, together, jb)
        for b in range(parts):
            out_ref[:, g * together : (g + 1) * together, b * jb : (b + 1) * jb] = (
                block[b] * scale_ref[:, b * jb : (b + 1) * jb][:, None, :]
            )


def jacobian(rows, features, signals, scaling, walkers, slots):
    sources, ib, lanes = features.shape
    jb = signals.shape[1]
    tiles = ib * jb // LANES
    per_source = lanes // slots
    return pl.pallas_call(
        functools.partial(jacobian_kernel, slots),
        out_shape=jax.ShapeDtypeStruct((tiles, walkers, LANES), jnp.float32),
        grid_spec=pltpu.PrefetchScalarGridSpec(
            num_scalar_prefetch=1,
            grid=(sources,),
            in_specs=[
                pl.BlockSpec((1, ib, lanes), lambda q, rows: (q, 0, 0)),
                pl.BlockSpec((1, jb, lanes), lambda q, rows: (q, 0, 0)),
                pl.BlockSpec((tiles, LANES), lambda q, rows: (0, 0)),
            ],
            out_specs=pl.BlockSpec((tiles, per_source, LANES), lambda q, rows: (0, rows[q], 0)),
        ),
        compiler_params=pltpu.CompilerParams(vmem_limit_bytes=VMEM_LIMIT),
        name="jacobian",
    )(rows, features, signals, scaling)


def split_two(value):
    high = value.astype(jnp.bfloat16)
    return high, (value - high.astype(jnp.float32)).astype(jnp.bfloat16)


def gram_kernel(
    row_block, col_block, orders, row_at, col_at, j_ref, hot_ref, hot_t_ref, recip_ref, a_ref, b_ref, high_ref, low_ref
):
    @pl.when(pl.program_id(0) == 0)
    def _():
        a_ref[...] = jnp.zeros_like(a_ref)
        b_ref[...] = jnp.zeros_like(b_ref)

    value = j_ref[0]
    high, low = split_two(value)
    dot = functools.partial(jnp.dot, preferred_element_type=jnp.float32)
    means = (dot(hot_t_ref[...], high) + dot(hot_t_ref[...], low)) * recip_ref[...]
    first, rest = split_two(means)
    second, third = split_two(means - first.astype(jnp.float32))
    hot = hot_ref[...]
    value = value - (dot(hot, first) + dot(hot, second))
    del rest, third
    high, low = split_two(value)
    high_ref[...] = high
    low_ref[...] = low
    slots = len(orders[0])
    left = []
    for s in range(slots):
        at = pl.ds(pl.multiple_of(row_at[s], 16), row_block)
        h, l = high_ref[at, :], low_ref[at, :]
        left.append(jnp.concatenate([h, h, l], axis=1))
    left = jnp.concatenate(left, axis=0)
    blocks = col_at.shape[0]
    for half, out in enumerate((a_ref, b_ref)):
        for n in range(blocks // 2):
            at = pl.ds(pl.multiple_of(col_at[half * (blocks // 2) + n], 16), col_block)
            h, l = high_ref[at, :], low_ref[at, :]
            right = jnp.concatenate([h, l, h], axis=1)
            got = lax.dot_general(left, right, CONTRACT_LAST, preferred_element_type=jnp.float32)
            for place, s in enumerate(orders[half]):
                out[place * row_block : (place + 1) * row_block, n * col_block : (n + 1) * col_block] += got[
                    s * row_block : (s + 1) * row_block
                ]


def gram_rows(columns, hot, hot_t, recip, row_at, col_at, row_block, col_block, orders):
    tiles, walkers, lanes = columns.shape
    groups = hot.shape[1]
    slots = len(orders[0])
    half = jax.ShapeDtypeStruct((slots * row_block, walkers // 2), jnp.float32)
    fixed = lambda t, r, c: (0, 0)
    return pl.pallas_call(
        functools.partial(gram_kernel, row_block, col_block, orders),
        out_shape=(half, half),
        grid_spec=pltpu.PrefetchScalarGridSpec(
            num_scalar_prefetch=2,
            grid=(tiles,),
            in_specs=[
                pl.BlockSpec((1, walkers, lanes), lambda t, r, c: (t, 0, 0)),
                pl.BlockSpec((walkers, groups), fixed),
                pl.BlockSpec((groups, walkers), fixed),
                pl.BlockSpec((groups, 1), fixed),
            ],
            out_specs=(pl.BlockSpec(half.shape, fixed), pl.BlockSpec(half.shape, fixed)),
            scratch_shapes=[
                pltpu.VMEM((walkers, lanes), jnp.bfloat16),
                pltpu.VMEM((walkers, lanes), jnp.bfloat16),
            ],
        ),
        compiler_params=pltpu.CompilerParams(vmem_limit_bytes=VMEM_LIMIT),
        name="gram_rows",
    )(row_at, col_at, columns, hot, hot_t, recip)


def on_device(features, signals, param_scale, geometry, electrons):
    par_size = lax.axis_size("par")
    walk_size = lax.axis_size("walk")
    walk_index = lax.axis_index("walk")
    par_index = lax.axis_index("par")
    per_device, slots_count, width = features.shape
    walkers = geometry.shape[0]
    groups = electrons.shape[0]
    row_block = per_device * par_size
    col_block = walkers // par_size
    plan = Plan(walk_size, par_size)

    anchor = (walk_index * par_size + par_index) * per_device
    own_geometry = lax.dynamic_slice_in_dim(geometry, anchor, per_device)
    own_matches = own_geometry[:, None] == jnp.arange(groups, dtype=jnp.int32)[None, :]
    own_electrons = jnp.sum(jnp.where(own_matches, electrons[None, :], 0), axis=1)
    live = jnp.arange(slots_count, dtype=jnp.int32)[None, :] < own_electrons[:, None]
    masked = jnp.where(live[:, :, None], features, jnp.zeros_like(features))

    own = {"F": 0, "S": 0}
    for k, (axis, bit, kind) in enumerate(plan.dims):
        index = walk_index if axis == "walk" else par_index
        side = "F" if kind == "I" else "S"
        own[side] = own[side] + jnp.where((index & bit) != 0, 1 << plan.place[k], 0)
    pieces = {}
    for side, value in (("F", masked), ("S", signals)):
        flat = value.reshape(per_device * slots_count, width).T.astype(jnp.float32)
        size = width // plan.blocks[side]
        for rb in range(plan.blocks[side]):
            pieces[side, 0, rb] = lax.dynamic_slice_in_dim(flat, (own[side] ^ rb) * size, size, 0)
    ib, jb = width // plan.blocks["F"], width // plan.blocks["S"]
    stacks = exchange(plan, pieces)
    left, left_names = gathered(stacks["F"], None)
    right, right_names = gathered(stacks["S"], None)
    if left_names != right_names:
        right = jnp.concatenate(
            [right[i : i + 1] for i in [right_names.index(n) for n in left_names]], axis=0
        )
    rows = []
    for src, core in left_names:
        walk_flip, par_flip = plan.flip(src)
        rows.append((walk_index ^ (walk_flip | core)) * par_size + (par_index ^ par_flip))
    rows = jnp.stack(rows).astype(jnp.int32)

    parts = LANES // jb
    scaling = param_scale * (1.0 / math.sqrt(slots_count * width * width))
    scaling = lax.dynamic_slice(scaling, (own["F"] * ib, own["S"] * jb), (ib, jb))
    scaling = scaling.reshape(parts, ib // parts, jb).transpose(1, 0, 2).reshape(ib // parts, LANES)
    columns = jacobian(rows, left, right, scaling, walkers, slots_count)

    matches = geometry[:, None] == jnp.arange(groups, dtype=jnp.int32)[None, :]
    hot = matches.astype(jnp.bfloat16)
    hot_t = (jnp.arange(groups, dtype=jnp.int32)[:, None] == geometry[None, :]).astype(jnp.bfloat16)
    counts = jnp.maximum(jnp.sum(matches.astype(jnp.float32), axis=0), 1.0)
    recip = (1.0 / counts)[:, None]

    chip_bits = walk_size.bit_length() - 2
    slots = 1 << chip_bits
    core, chip = walk_index & 1, walk_index >> 1
    row_at = jnp.stack([((chip ^ s) * 2 + core) * row_block for s in range(slots)]).astype(jnp.int32)
    col_at = jnp.stack([(par_index ^ p) * col_block for p in range(par_size)]).astype(jnp.int32)
    up = list(range(chip_bits))
    sweeps = (up, up[::-1])
    orders = tuple(
        tuple(sorted(range(slots), key=lambda s, o=o: [s >> b & 1 for b in o])) for o in sweeps
    )
    halves = list(gram_rows(columns, hot, hot_t, recip, row_at, col_at, row_block, col_block, orders))
    for step in range(chip_bits):
        moved = []
        for h in range(2):
            mid = halves[h].shape[0] // 2
            bit = 2 << sweeps[h][step]
            moved.append(permute(halves[h][mid:], "walk", walk_size, bit))
        halves = [halves[h][: halves[h].shape[0] // 2] + moved[h] for h in range(2)]
    gram = halves[0] + permute(halves[1], "par", par_size, par_size // 2)
    bit = par_size // 4
    while bit:
        mid = gram.shape[1] // 2
        gram = gram[:, :mid] + permute(gram[:, mid:], "par", par_size, bit)
        bit //= 2

    row_ids = walk_index * row_block + jnp.arange(row_block, dtype=jnp.int32)
    col_ids = par_index * col_block + jnp.arange(col_block, dtype=jnp.int32)
    shifted = gram + SHIFT * (row_ids[:, None] == col_ids[None, :]).astype(jnp.float32)
    whole_rows = lax.all_gather(shifted, "par", axis=1, tiled=True)
    panel_part = whole_rows[:, :PB]
    panel_whole = lax.all_gather(panel_part, "walk", axis=0, tiled=True)
    factor_head = jnp.linalg.cholesky(panel_whole[:PB])
    head_inverse = jax.scipy.linalg.solve_triangular(
        factor_head, jnp.eye(PB, dtype=jnp.float32), lower=True
    )
    own_panel = outer_rows(panel_part, head_inverse)
    col_rows = lax.dynamic_slice_in_dim(panel_whole, par_index * col_block, col_block, 0)
    col_panel = outer_rows(col_rows, head_inverse)
    trailing = shifted - outer_rows(own_panel, col_panel)
    return (own_panel, trailing)


def solution(mesh):
    in_specs = (P(("walk", "par"), None, None), P(("walk", "par"), None, None), P(), P(), P())
    out_specs = (P("walk", None), P("walk", "par"))
    return jax.shard_map(
        on_device, mesh=mesh, in_specs=in_specs, out_specs=out_specs, check_vma=False
    )
```

```python
import functools
import math

import jax
import jax.numpy as jnp
import numpy as np
from jax import lax
from jax.experimental import pallas as pl
from jax.experimental.pallas import tpu as pltpu
from jax.sharding import PartitionSpec as P

PB = 256
HIGHEST = lax.Precision.HIGHEST
SHIFT = 0.05
LANES = 256
CONTRACT_LAST = (((1,), (1,)), ((), ()))
VMEM_LIMIT = 60 * 1024 * 1024


def outer_rows(left_rows, right_rows):
    return lax.dot_general(left_rows, right_rows, CONTRACT_LAST, precision=HIGHEST)


def xor_pairs(size, bit):
    return [(i, i ^ bit) for i in range(size)]


class Plan:
    def __init__(self, walk_size, par_size):
        self.walk_size, self.par_size = walk_size, par_size
        par_bits = par_size.bit_length() - 1
        walk_bits = walk_size.bit_length() - 1
        self.dims = []
        for bit in reversed(range(par_bits)):
            self.dims.append(("par", 1 << bit, "J" if bit == 0 else "I"))
        for bit in range(1, walk_bits):
            self.dims.append(("walk", 1 << bit, "J" if bit == walk_bits - 1 else "I"))
        self.place = []
        seen = {"I": 0, "J": 0}
        for _, _, kind in self.dims:
            self.place.append(seen[kind])
            seen[kind] += 1
        self.blocks = {"F": 1 << seen["I"], "S": 1 << seen["J"]}
        self.order = {
            side: sorted(
                range(len(self.dims)), key=lambda k: (self.dims[k][0] == "walk", not self.splits(side, self.dims[k][2]))
            )
            for side in ("F", "S")
        }
        self.rounds = self.schedule()

    def splits(self, side, kind):
        return (side == "F") == (kind == "I")

    def depth(self, side, src, rb, after):
        best = 0
        order = self.order[side]
        for k in order[order.index(after) + 1 :]:
            if self.splits(side, self.dims[k][2]):
                if rb >> self.place[k] & 1:
                    return max(best, 1 + self.depth(side, src, rb ^ (1 << self.place[k]), k))
            else:
                best = max(best, 1 + self.depth(side, src, rb, k))
        return best

    def tasks(self):
        out = []
        for side in ("F", "S"):
            live = [(0, rb) for rb in range(self.blocks[side])]
            for k in self.order[side]:
                kind = self.dims[k][2]
                kept, made = [], []
                for src, rb in live:
                    if self.splits(side, kind):
                        p = self.place[k]
                        if rb >> p & 1:
                            made.append((k, (side, src, rb), (side, src | 1 << k, rb ^ (1 << p))))
                        else:
                            kept.append((src, rb))
                    else:
                        kept.append((src, rb))
                        made.append((k, (side, src, rb), (side, src | 1 << k, rb)))
                live = kept + [dst[1:] for _, _, dst in made]
                out += made
        return out

    def schedule(self):
        left = self.tasks()
        have = {(side, 0, rb) for side in ("F", "S") for rb in range(self.blocks[side])}
        rounds = []
        while left:
            chosen = []
            for k, (axis, _, _) in enumerate(self.dims):
                ready = [t for t in left if t[0] == k and t[1] in have]
                ready.sort(
                    key=lambda t: (
                        not self.splits(t[1][0], self.dims[k][2]),
                        -self.depth(*t[2], k),
                    )
                )
                chosen += ready[: 1 if axis == "par" else 2]
            left = [t for t in left if t not in chosen]
            have |= {t[2] for t in chosen}
            rounds.append(chosen)
        return rounds

    def flip(self, src):
        walk = par = 0
        for k, (axis, bit, _) in enumerate(self.dims):
            if src >> k & 1:
                walk, par = (walk | bit, par) if axis == "walk" else (walk, par | bit)
        return walk, par


def permute(value, axis, size, bit):
    return lax.ppermute(value, axis, xor_pairs(size, bit))


def exchange(plan, pieces, block):
    sizes = {"walk": plan.walk_size, "par": plan.par_size}
    held = dict(pieces)
    planes, chips = plan.par_size, plan.walk_size // 2
    members = {q: [q | m * planes for m in range(chips)] for q in range(planes)}
    waiting = list(range(planes))
    own, other, sent = {}, {}, []
    gate = []
    rounds = list(plan.rounds)
    while rounds or waiting or sent:
        chosen = rounds.pop(0) if rounds else []
        groups = {}
        for k, src, dst in chosen:
            groups.setdefault((k, held[src].shape), []).append((src, dst))
        keys = sorted({s for pairs in groups.values() for s, _ in pairs})
        if gate and keys:
            tied = lax.optimization_barrier(tuple(held[n] for n in keys) + tuple(held[n] for n in gate))
            for n, v in zip(keys + gate, tied):
                held[n] = v
        gate = []
        for q in sent:
            other[q] = permute(own[q], "walk", plan.walk_size, 1)
        sent = []
        for q in list(waiting):
            if all((side, m, 0) in held for side in ("F", "S") for m in members[q]):
                own[q] = block([held["F", m, 0] for m in members[q]], [held["S", m, 0] for m in members[q]])
                waiting.remove(q)
                sent.append(q)
        for (k, _), pairs in groups.items():
            axis, bit, _ = plan.dims[k]
            if len(pairs) == 1:
                held[pairs[0][1]] = permute(held[pairs[0][0]], axis, sizes[axis], bit)
            else:
                moved = permute(jnp.stack([held[s] for s, _ in pairs]), axis, sizes[axis], bit)
                for i, (_, d) in enumerate(pairs):
                    held[d] = moved[i]
            gate += [d for _, d in pairs]
    return [own[q] for q in range(planes)] + [other[q] for q in range(planes)], [
        [(m, core) for m in members[q]] for core in range(2) for q in range(planes)
    ]


def jacobian_kernel(slots, count, *refs):
    lefts, rights, scale_ref, out_ref = refs[:count], refs[count : 2 * count], refs[2 * count], refs[-1]
    ib = lefts[0].shape[0]
    jb = rights[0].shape[0]
    together = LANES // slots
    parts = LANES // jb
    lane = lax.broadcasted_iota(jnp.int32, (together, LANES), 1)
    row = lax.broadcasted_iota(jnp.int32, (together, LANES), 0)
    mine = (lane >= row * slots) & (lane < row * slots + slots)
    for n in range(count):
        left = lefts[n][...]
        right = rights[n][...].astype(jnp.bfloat16)
        spread = jnp.where(mine[None], left[:, None, :], 0.0).reshape(ib * together, LANES)
        block = lax.dot_general(
            spread.astype(jnp.bfloat16), right, CONTRACT_LAST, preferred_element_type=jnp.float32
        )
        block = block.reshape(parts, ib // parts, together, jb)
        for b in range(parts):
            out_ref[:, n, :, b * jb : (b + 1) * jb] = block[b] * scale_ref[:, b * jb : (b + 1) * jb][:, None, :]


def jacobian(lefts, rights, scaling, slots):
    count = len(lefts)
    ib, lanes = lefts[0].shape
    jb = rights[0].shape[0]
    tiles = ib * jb // LANES
    together = LANES // slots
    return pl.pallas_call(
        functools.partial(jacobian_kernel, slots, count),
        out_shape=jax.ShapeDtypeStruct((tiles, count, lanes // slots, LANES), jnp.float32),
        grid=(lanes // LANES,),
        in_specs=[pl.BlockSpec((ib, LANES), lambda g: (0, g))] * count
        + [pl.BlockSpec((jb, LANES), lambda g: (0, g))] * count
        + [pl.BlockSpec((tiles, LANES), lambda g: (0, 0))],
        out_specs=pl.BlockSpec((tiles, count, together, LANES), lambda g: (0, 0, g, 0)),
        compiler_params=pltpu.CompilerParams(vmem_limit_bytes=VMEM_LIMIT),
        name="jacobian",
    )(*lefts, *rights, scaling)


def split_two(value):
    high = value.astype(jnp.bfloat16)
    return high, (value - high.astype(jnp.float32)).astype(jnp.bfloat16)


def gram_kernel(row_block, col_block, orders, count, row_at, col_at, place_at, *refs):
    pieces = refs[:count]
    hot_ref, hot_t_ref, recip_ref, a_ref, b_ref, value_ref, high_ref, low_ref = refs[count:]

    @pl.when(pl.program_id(0) == 0)
    def _():
        a_ref[...] = jnp.zeros_like(a_ref)
        b_ref[...] = jnp.zeros_like(b_ref)

    members, rows = pieces[0].shape[1:3]
    for a in range(count):
        for m in range(members):
            value_ref[pl.ds(pl.multiple_of(place_at[a * members + m], 8), rows), :] = pieces[a][0, m]
    value = value_ref[...]
    high, low = split_two(value)
    dot = functools.partial(jnp.dot, preferred_element_type=jnp.float32)
    means = (dot(hot_t_ref[...], high) + dot(hot_t_ref[...], low)) * recip_ref[...]
    first, second = split_two(means)
    hot = hot_ref[...]
    high, low = split_two(value - (dot(hot, first) + dot(hot, second)))
    high_ref[...] = high
    low_ref[...] = low
    blocks = col_at.shape[0]
    for half, out in enumerate((a_ref, b_ref)):
        left = []
        for s in orders[half]:
            at = pl.ds(pl.multiple_of(row_at[s], 16), row_block)
            h, l = high_ref[at, :], low_ref[at, :]
            left.append(jnp.concatenate([h, h, l], axis=1))
        left = jnp.concatenate(left, axis=0)
        right = []
        for n in range(blocks // 2):
            at = pl.ds(pl.multiple_of(col_at[half * (blocks // 2) + n], 16), col_block)
            h, l = high_ref[at, :], low_ref[at, :]
            right.append(jnp.concatenate([h, l, h], axis=1))
        right = jnp.concatenate(right, axis=0)
        out[...] += lax.dot_general(left, right, CONTRACT_LAST, preferred_element_type=jnp.float32)


def gram_rows(pieces, hot, hot_t, recip, row_at, col_at, place_at, row_block, col_block, orders):
    tiles, members, rows, lanes = pieces[0].shape
    walkers, groups = hot.shape
    slots = len(orders[0])
    half = jax.ShapeDtypeStruct((slots * row_block, walkers // 2), jnp.float32)
    fixed = lambda t, *_: (0, 0)
    return pl.pallas_call(
        functools.partial(gram_kernel, row_block, col_block, orders, len(pieces)),
        out_shape=(half, half),
        grid_spec=pltpu.PrefetchScalarGridSpec(
            num_scalar_prefetch=3,
            grid=(tiles,),
            in_specs=[pl.BlockSpec((1, members, rows, lanes), lambda t, *_: (t, 0, 0, 0))] * len(pieces)
            + [
                pl.BlockSpec((walkers, groups), fixed),
                pl.BlockSpec((groups, walkers), fixed),
                pl.BlockSpec((groups, 1), fixed),
            ],
            out_specs=(pl.BlockSpec(half.shape, fixed), pl.BlockSpec(half.shape, fixed)),
            scratch_shapes=[
                pltpu.VMEM((walkers, lanes), jnp.float32),
                pltpu.VMEM((walkers, lanes), jnp.bfloat16),
                pltpu.VMEM((walkers, lanes), jnp.bfloat16),
            ],
        ),
        compiler_params=pltpu.CompilerParams(vmem_limit_bytes=VMEM_LIMIT),
        name="gram_rows",
    )(row_at, col_at, place_at, *pieces, hot, hot_t, recip)


def on_device(features, signals, param_scale, geometry, electrons):
    par_size = lax.axis_size("par")
    walk_size = lax.axis_size("walk")
    walk_index = lax.axis_index("walk")
    par_index = lax.axis_index("par")
    per_device, slots_count, width = features.shape
    walkers = geometry.shape[0]
    groups = electrons.shape[0]
    row_block = per_device * par_size
    col_block = walkers // par_size
    plan = Plan(walk_size, par_size)

    anchor = (walk_index * par_size + par_index) * per_device
    own_geometry = lax.dynamic_slice_in_dim(geometry, anchor, per_device)
    own_matches = own_geometry[:, None] == jnp.arange(groups, dtype=jnp.int32)[None, :]
    own_electrons = jnp.sum(jnp.where(own_matches, electrons[None, :], 0), axis=1)
    live = jnp.arange(slots_count, dtype=jnp.int32)[None, :] < own_electrons[:, None]
    masked = jnp.where(live[:, :, None], features, jnp.zeros_like(features))

    own = {"F": 0, "S": 0}
    for k, (axis, bit, kind) in enumerate(plan.dims):
        index = walk_index if axis == "walk" else par_index
        side = "F" if kind == "I" else "S"
        own[side] = own[side] + jnp.where((index & bit) != 0, 1 << plan.place[k], 0)
    pieces = {}
    for side, value in (("F", masked), ("S", signals)):
        flat = value.reshape(per_device * slots_count, width).T.astype(jnp.float32)
        size = width // plan.blocks[side]
        for rb in range(plan.blocks[side]):
            pieces[side, 0, rb] = lax.dynamic_slice_in_dim(flat, (own[side] ^ rb) * size, size, 0)
    ib, jb = width // plan.blocks["F"], width // plan.blocks["S"]
    parts = LANES // jb
    scaling = param_scale * (1.0 / math.sqrt(slots_count * width * width))
    scaling = lax.dynamic_slice(scaling, (own["F"] * ib, own["S"] * jb), (ib, jb))
    scaling = scaling.reshape(parts, ib // parts, jb).transpose(1, 0, 2).reshape(ib // parts, LANES)
    columns, names = exchange(plan, pieces, lambda f, s: jacobian(f, s, scaling, slots_count))
    place_at = []
    for src, core in [n for members in names for n in members]:
        walk_flip, par_flip = plan.flip(src)
        place_at.append((walk_index ^ (walk_flip | core)) * par_size + (par_index ^ par_flip))
    place_at = (jnp.stack(place_at) * per_device).astype(jnp.int32)

    matches = geometry[:, None] == jnp.arange(groups, dtype=jnp.int32)[None, :]
    hot = matches.astype(jnp.bfloat16)
    hot_t = (jnp.arange(groups, dtype=jnp.int32)[:, None] == geometry[None, :]).astype(jnp.bfloat16)
    counts = jnp.maximum(jnp.sum(matches.astype(jnp.float32), axis=0), 1.0)
    recip = (1.0 / counts)[:, None]

    chip_bits = walk_size.bit_length() - 2
    slots = 1 << chip_bits
    core, chip = walk_index & 1, walk_index >> 1
    row_at = jnp.stack([((chip ^ s) * 2 + core) * row_block for s in range(slots)]).astype(jnp.int32)
    col_at = jnp.stack([(par_index ^ p) * col_block for p in range(par_size)]).astype(jnp.int32)
    up = list(range(chip_bits))
    sweeps = (up, up[::-1])
    orders = tuple(
        tuple(sorted(range(slots), key=lambda s, o=o: [s >> b & 1 for b in o])) for o in sweeps
    )
    halves = list(gram_rows(columns, hot, hot_t, recip, row_at, col_at, place_at, row_block, col_block, orders))
    for step in range(chip_bits):
        moved = []
        for h in range(2):
            mid = halves[h].shape[0] // 2
            bit = 2 << sweeps[h][step]
            moved.append(permute(halves[h][mid:], "walk", walk_size, bit))
        halves = [halves[h][: halves[h].shape[0] // 2] + moved[h] for h in range(2)]
    gram = halves[0] + permute(halves[1], "par", par_size, par_size // 2)
    bit = par_size // 4
    while bit:
        mid = gram.shape[1] // 2
        gram = gram[:, :mid] + permute(gram[:, mid:], "par", par_size, bit)
        bit //= 2

    row_ids = walk_index * row_block + jnp.arange(row_block, dtype=jnp.int32)
    col_ids = par_index * col_block + jnp.arange(col_block, dtype=jnp.int32)
    shifted = gram + SHIFT * (row_ids[:, None] == col_ids[None, :]).astype(jnp.float32)
    whole_rows = lax.all_gather(shifted, "par", axis=1, tiled=True)
    panel_part = whole_rows[:, :PB]
    panel_whole = lax.all_gather(panel_part, "walk", axis=0, tiled=True)
    factor_head = jnp.linalg.cholesky(panel_whole[:PB])
    head_inverse = jax.scipy.linalg.solve_triangular(
        factor_head, jnp.eye(PB, dtype=jnp.float32), lower=True
    )
    own_panel = outer_rows(panel_part, head_inverse)
    col_rows = lax.dynamic_slice_in_dim(panel_whole, par_index * col_block, col_block, 0)
    col_panel = outer_rows(col_rows, head_inverse)
    trailing = shifted - outer_rows(own_panel, col_panel)
    return (own_panel, trailing)


def solution(mesh):
    in_specs = (P(("walk", "par"), None, None), P(("walk", "par"), None, None), P(), P(), P())
    out_specs = (P("walk", None), P("walk", "par"))
    return jax.shard_map(
        on_device, mesh=mesh, in_specs=in_specs, out_specs=out_specs, check_vma=False
    )
```

```python
import functools
import math

import jax
import jax.numpy as jnp
import numpy as np
from jax import lax
from jax.experimental import pallas as pl
from jax.experimental.pallas import tpu as pltpu
from jax.sharding import PartitionSpec as P

PB = 256
HIGHEST = lax.Precision.HIGHEST
SHIFT = 0.05
LANES = 256
SUB = 8
CONTRACT_LAST = (((1,), (1,)), ((), ()))
VMEM_LIMIT = 60 * 1024 * 1024


def outer_rows(left_rows, right_rows):
    return lax.dot_general(left_rows, right_rows, CONTRACT_LAST, precision=HIGHEST)


def xor_pairs(size, bit):
    return [(i, i ^ bit) for i in range(size)]


class Plan:
    def __init__(self, walk_size, par_size):
        self.walk_size, self.par_size = walk_size, par_size
        par_bits = par_size.bit_length() - 1
        walk_bits = walk_size.bit_length() - 1
        self.dims = []
        for bit in reversed(range(par_bits)):
            self.dims.append(("par", 1 << bit, "J" if bit == 0 else "I"))
        for bit in range(1, walk_bits):
            self.dims.append(("walk", 1 << bit, "J" if bit == walk_bits - 1 else "I"))
        self.place = []
        seen = {"I": 0, "J": 0}
        for _, _, kind in self.dims:
            self.place.append(seen[kind])
            seen[kind] += 1
        self.blocks = {"F": 1 << seen["I"], "S": 1 << seen["J"]}
        self.order = {
            side: sorted(
                range(len(self.dims)), key=lambda k: (self.dims[k][0] == "walk", not self.splits(side, self.dims[k][2]))
            )
            for side in ("F", "S")
        }
        self.rounds = self.schedule()

    def splits(self, side, kind):
        return (side == "F") == (kind == "I")

    def depth(self, side, src, rb, after):
        best = 0
        order = self.order[side]
        for k in order[order.index(after) + 1 :]:
            if self.splits(side, self.dims[k][2]):
                if rb >> self.place[k] & 1:
                    return max(best, 1 + self.depth(side, src, rb ^ (1 << self.place[k]), k))
            else:
                best = max(best, 1 + self.depth(side, src, rb, k))
        return best

    def tasks(self):
        out = []
        for side in ("F", "S"):
            live = [(0, rb) for rb in range(self.blocks[side])]
            for k in self.order[side]:
                kind = self.dims[k][2]
                kept, made = [], []
                for src, rb in live:
                    if self.splits(side, kind):
                        p = self.place[k]
                        if rb >> p & 1:
                            made.append((k, (side, src, rb), (side, src | 1 << k, rb ^ (1 << p))))
                        else:
                            kept.append((src, rb))
                    else:
                        kept.append((src, rb))
                        made.append((k, (side, src, rb), (side, src | 1 << k, rb)))
                live = kept + [dst[1:] for _, _, dst in made]
                out += made
        return out

    def schedule(self):
        left = self.tasks()
        have = {(side, 0, rb) for side in ("F", "S") for rb in range(self.blocks[side])}
        rounds = []
        while left:
            chosen = []
            for k, (axis, _, _) in enumerate(self.dims):
                ready = [t for t in left if t[0] == k and t[1] in have]
                ready.sort(
                    key=lambda t: (
                        not self.splits(t[1][0], self.dims[k][2]),
                        axis == "par" and (t[2][1] & (self.par_size - 1)).bit_count(),
                        -self.depth(*t[2], k),
                    )
                )
                chosen += ready[: 1 if axis == "par" else 2]
            left = [t for t in left if t not in chosen]
            have |= {t[2] for t in chosen}
            rounds.append(chosen)
        return rounds

    def flip(self, src):
        walk = par = 0
        for k, (axis, bit, _) in enumerate(self.dims):
            if src >> k & 1:
                walk, par = (walk | bit, par) if axis == "walk" else (walk, par | bit)
        return walk, par


def permute(value, axis, size, bit):
    return lax.ppermute(value, axis, xor_pairs(size, bit))


def exchange(plan, pieces, block):
    sizes = {"walk": plan.walk_size, "par": plan.par_size}
    held = dict(pieces)
    planes, chips = plan.par_size, plan.walk_size // 2
    members = {q: [q | m * planes for m in range(chips)] for q in range(planes)}
    waiting = list(range(planes))
    own, other, sent = {}, {}, []
    gate = []
    rounds = list(plan.rounds)
    while rounds or waiting or sent:
        chosen = rounds.pop(0) if rounds else []
        groups = {}
        for k, src, dst in chosen:
            groups.setdefault((k, held[src].shape), []).append((src, dst))
        keys = sorted({s for pairs in groups.values() for s, _ in pairs})
        if gate and keys:
            tied = lax.optimization_barrier(tuple(held[n] for n in keys) + tuple(held[n] for n in gate))
            for n, v in zip(keys + gate, tied):
                held[n] = v
        gate = []
        if sent and keys:
            tied = lax.optimization_barrier(tuple(held[n] for n in keys) + tuple(own[q] for q in sent))
            for n, v in zip(keys, tied):
                held[n] = v
            for q, v in zip(sent, tied[len(keys) :]):
                own[q] = v
        for q in sent:
            other[q] = permute(own[q], "walk", plan.walk_size, 1)
        sent = []
        for q in list(waiting):
            if all((side, m, 0) in held for side in ("F", "S") for m in members[q]):
                own[q] = block([held["F", m, 0] for m in members[q]], [held["S", m, 0] for m in members[q]])
                waiting.remove(q)
                sent.append(q)
        for (k, _), pairs in groups.items():
            axis, bit, _ = plan.dims[k]
            if len(pairs) == 1:
                held[pairs[0][1]] = permute(held[pairs[0][0]], axis, sizes[axis], bit)
            else:
                moved = permute(jnp.stack([held[s] for s, _ in pairs]), axis, sizes[axis], bit)
                for i, (_, d) in enumerate(pairs):
                    held[d] = moved[i]
            gate += [d for _, d in pairs]
    return [own[q] for q in range(planes)] + [other[q] for q in range(planes)], [
        [(m, core) for m in members[q]] for core in range(2) for q in range(planes)
    ]


def jacobian_kernel(slots, count, *refs):
    lefts, rights, scale_ref, out_ref = refs[:count], refs[count : 2 * count], refs[2 * count], refs[-1]
    ib = lefts[0].shape[0]
    jb = rights[0].shape[0]
    together = LANES // slots
    parts = LANES // jb
    lane = lax.broadcasted_iota(jnp.int32, (together, LANES), 1)
    row = lax.broadcasted_iota(jnp.int32, (together, LANES), 0)
    mine = (lane >= row * slots) & (lane < row * slots + slots)
    for n in range(count):
        left = lefts[n][...]
        right = rights[n][...].astype(jnp.bfloat16)
        spread = jnp.where(mine[None], left[:, None, :], 0.0).reshape(ib * together, LANES)
        block = lax.dot_general(
            spread.astype(jnp.bfloat16), right, CONTRACT_LAST, preferred_element_type=jnp.float32
        )
        block = block.reshape(parts, ib // parts, together, jb)
        for b in range(parts):
            out_ref[:, n, :, b * jb : (b + 1) * jb] = block[b] * scale_ref[:, b * jb : (b + 1) * jb][:, None, :]


def jacobian(lefts, rights, scaling, slots):
    count = len(lefts)
    ib, lanes = lefts[0].shape
    jb = rights[0].shape[0]
    tiles = ib * jb // LANES
    together = LANES // slots
    return pl.pallas_call(
        functools.partial(jacobian_kernel, slots, count),
        out_shape=jax.ShapeDtypeStruct((tiles, count, lanes // slots, LANES), jnp.float32),
        grid=(lanes // LANES,),
        in_specs=[pl.BlockSpec((ib, LANES), lambda g: (0, g))] * count
        + [pl.BlockSpec((jb, LANES), lambda g: (0, g))] * count
        + [pl.BlockSpec((tiles, LANES), lambda g: (0, 0))],
        out_specs=pl.BlockSpec((tiles, count, together, LANES), lambda g: (0, 0, g, 0)),
        compiler_params=pltpu.CompilerParams(vmem_limit_bytes=VMEM_LIMIT),
        name="jacobian",
    )(*lefts, *rights, scaling)


def split_two(value):
    high = value.astype(jnp.bfloat16)
    return high, (value - high.astype(jnp.float32)).astype(jnp.bfloat16)


def gram_kernel(row_block, col_block, orders, count, row_at, col_at, place_at, *refs):
    pieces = refs[:count]
    hot_ref, hot_t_ref, recip_ref, a_ref, b_ref, value_ref, high_ref, low_ref = refs[count:]

    @pl.when(pl.program_id(0) == 0)
    def _():
        a_ref[...] = jnp.zeros_like(a_ref)
        b_ref[...] = jnp.zeros_like(b_ref)

    members, rows = pieces[0].shape[1:3]
    for a in range(count):
        for m in range(members):
            value_ref[pl.ds(pl.multiple_of(place_at[a * members + m], 8), rows), :] = pieces[a][0, m]
    value = value_ref[...]
    high, low = split_two(value)
    dot = functools.partial(jnp.dot, preferred_element_type=jnp.float32)
    means = (dot(hot_t_ref[...], high) + dot(hot_t_ref[...], low)) * recip_ref[...]
    first, second = split_two(means)
    hot = hot_ref[...]
    high, low = split_two(value - (dot(hot, first) + dot(hot, second)))
    high_ref[...] = high
    low_ref[...] = low
    blocks = col_at.shape[0]
    for half, out in enumerate((a_ref, b_ref)):
        left = []
        for s in orders[half]:
            at = pl.ds(pl.multiple_of(row_at[s], 16), row_block)
            h, l = high_ref[at, :], low_ref[at, :]
            left.append(jnp.concatenate([h, h, l], axis=1))
        left = jnp.concatenate(left, axis=0)
        right = []
        for n in range(blocks // 2):
            at = pl.ds(pl.multiple_of(col_at[half * (blocks // 2) + n], 16), col_block)
            h, l = high_ref[at, :], low_ref[at, :]
            right.append(jnp.concatenate([h, l, h], axis=1))
        right = jnp.concatenate(right, axis=0)
        out[...] += lax.dot_general(left, right, CONTRACT_LAST, preferred_element_type=jnp.float32)


def gram_rows(pieces, hot, hot_t, recip, row_at, col_at, place_at, row_block, col_block, orders):
    tiles, members, rows, lanes = pieces[0].shape
    walkers, groups = hot.shape
    slots = len(orders[0])
    half = jax.ShapeDtypeStruct((slots * row_block, walkers // 2), jnp.float32)
    fixed = lambda t, *_: (0, 0)
    return pl.pallas_call(
        functools.partial(gram_kernel, row_block, col_block, orders, len(pieces)),
        out_shape=(half, half),
        grid_spec=pltpu.PrefetchScalarGridSpec(
            num_scalar_prefetch=3,
            grid=(tiles,),
            in_specs=[pl.BlockSpec((1, members, rows, lanes), lambda t, *_: (t, 0, 0, 0))] * len(pieces)
            + [
                pl.BlockSpec((walkers, groups), fixed),
                pl.BlockSpec((groups, walkers), fixed),
                pl.BlockSpec((groups, 1), fixed),
            ],
            out_specs=(pl.BlockSpec(half.shape, fixed), pl.BlockSpec(half.shape, fixed)),
            scratch_shapes=[
                pltpu.VMEM((walkers, lanes), jnp.float32),
                pltpu.VMEM((walkers, lanes), jnp.bfloat16),
                pltpu.VMEM((walkers, lanes), jnp.bfloat16),
            ],
        ),
        compiler_params=pltpu.CompilerParams(vmem_limit_bytes=VMEM_LIMIT),
        name="gram_rows",
    )(row_at, col_at, place_at, *pieces, hot, hot_t, recip)


def inverse_factor(value):
    size = value.shape[0]
    lane = lax.broadcasted_iota(jnp.int32, (1, size), 1)
    sub = lax.broadcasted_iota(jnp.int32, (SUB, 1), 0)
    tiles = [value[t * SUB : (t + 1) * SUB] for t in range(size // SUB)]
    for j in range(size):
        home, at = divmod(j, SUB)
        row = tiles[home][at : at + 1]
        scaled = jnp.where(lane == j, 1.0, row) / row[:, j : j + 1]
        for t in range(home, len(tiles)):
            tile = tiles[t]
            factor = tile[:, j : j + 1]
            clear = lane == j
            if t == home:
                if at == SUB - 1:
                    continue
                factor = jnp.where(sub > at, factor, 0.0)
                clear = clear & (sub > at)
            tiles[t] = jnp.where(clear, 0.0, tile) - factor * scaled
    value = jnp.concatenate(tiles, axis=0)
    row_id = lax.broadcasted_iota(jnp.int32, (size, 1), 0)
    diagonal = jnp.sum(jnp.where(lane == row_id, value, 0.0), axis=1, keepdims=True)
    unit = jnp.where(lane < row_id, value, jnp.where(lane == row_id, 1.0, 0.0))
    return unit / jnp.sqrt(diagonal)


def head_kernel(a_ref, out_ref, work_ref, below_ref):
    half = work_ref.shape[0]
    dot = functools.partial(lax.dot_general, precision=HIGHEST, preferred_element_type=jnp.float32)
    first = pl.program_id(0) == 0
    @pl.when(first)
    def _():
        work_ref[...] = a_ref[:half, :half]
    inverse = inverse_factor(work_ref[...])
    @pl.when(first)
    def _():
        out_ref[:half, :half] = inverse
        out_ref[:half, half:] = jnp.zeros((half, half), jnp.float32)
        below = dot(a_ref[half:, :half], inverse, CONTRACT_LAST)
        below_ref[...] = below
        work_ref[...] = a_ref[half:, half:] - dot(below, below, CONTRACT_LAST)
    @pl.when(jnp.logical_not(first))
    def _():
        out_ref[half:, half:] = inverse
        plain = (((1,), (0,)), ((), ()))
        out_ref[half:, :half] = -dot(inverse, dot(below_ref[...], out_ref[:half, :half], plain), plain)


def head_inverse(head):
    size = head.shape[0]
    fixed = pl.BlockSpec((size, size), lambda i: (0, 0))
    return pl.pallas_call(
        head_kernel,
        out_shape=jax.ShapeDtypeStruct(head.shape, jnp.float32),
        grid=(2,),
        in_specs=[fixed],
        out_specs=fixed,
        scratch_shapes=[pltpu.VMEM((size // 2, size // 2), jnp.float32)] * 2,
        name="head_inverse",
    )(head)


def on_device(features, signals, param_scale, geometry, electrons):
    par_size = lax.axis_size("par")
    walk_size = lax.axis_size("walk")
    walk_index = lax.axis_index("walk")
    par_index = lax.axis_index("par")
    per_device, slots_count, width = features.shape
    walkers = geometry.shape[0]
    groups = electrons.shape[0]
    row_block = per_device * par_size
    col_block = walkers // par_size
    plan = Plan(walk_size, par_size)

    anchor = (walk_index * par_size + par_index) * per_device
    own_geometry = lax.dynamic_slice_in_dim(geometry, anchor, per_device)
    own_matches = own_geometry[:, None] == jnp.arange(groups, dtype=jnp.int32)[None, :]
    own_electrons = jnp.sum(jnp.where(own_matches, electrons[None, :], 0), axis=1)
    live = jnp.arange(slots_count, dtype=jnp.int32)[None, :] < own_electrons[:, None]
    masked = jnp.where(live[:, :, None], features, jnp.zeros_like(features))

    own = {"F": 0, "S": 0}
    for k, (axis, bit, kind) in enumerate(plan.dims):
        index = walk_index if axis == "walk" else par_index
        side = "F" if kind == "I" else "S"
        own[side] = own[side] + jnp.where((index & bit) != 0, 1 << plan.place[k], 0)
    pieces = {}
    for side, value in (("F", masked), ("S", signals)):
        flat = value.reshape(per_device * slots_count, width).T.astype(jnp.float32)
        size = width // plan.blocks[side]
        for rb in range(plan.blocks[side]):
            pieces[side, 0, rb] = lax.dynamic_slice_in_dim(flat, (own[side] ^ rb) * size, size, 0)
    ib, jb = width // plan.blocks["F"], width // plan.blocks["S"]
    parts = LANES // jb
    scaling = param_scale * (1.0 / math.sqrt(slots_count * width * width))
    scaling = lax.dynamic_slice(scaling, (own["F"] * ib, own["S"] * jb), (ib, jb))
    scaling = scaling.reshape(parts, ib // parts, jb).transpose(1, 0, 2).reshape(ib // parts, LANES)
    columns, names = exchange(plan, pieces, lambda f, s: jacobian(f, s, scaling, slots_count))
    place_at = []
    for src, core in [n for members in names for n in members]:
        walk_flip, par_flip = plan.flip(src)
        place_at.append((walk_index ^ (walk_flip | core)) * par_size + (par_index ^ par_flip))
    place_at = (jnp.stack(place_at) * per_device).astype(jnp.int32)

    matches = geometry[:, None] == jnp.arange(groups, dtype=jnp.int32)[None, :]
    hot = matches.astype(jnp.bfloat16)
    hot_t = (jnp.arange(groups, dtype=jnp.int32)[:, None] == geometry[None, :]).astype(jnp.bfloat16)
    counts = jnp.maximum(jnp.sum(matches.astype(jnp.float32), axis=0), 1.0)
    recip = (1.0 / counts)[:, None]

    chip_bits = walk_size.bit_length() - 2
    slots = 1 << chip_bits
    core, chip = walk_index & 1, walk_index >> 1
    row_at = jnp.stack([((chip ^ s) * 2 + core) * row_block for s in range(slots)]).astype(jnp.int32)
    col_at = jnp.stack([(par_index ^ p) * col_block for p in range(par_size)]).astype(jnp.int32)
    up = list(range(chip_bits))
    sweeps = (up, up[::-1])
    orders = tuple(
        tuple(sorted(range(slots), key=lambda s, o=o: [s >> b & 1 for b in o])) for o in sweeps
    )
    halves = list(gram_rows(columns, hot, hot_t, recip, row_at, col_at, place_at, row_block, col_block, orders))

    heads = []
    for h in range(2):
        part = lax.dynamic_slice(
            halves[h], (0, (par_index % (par_size // 2)) * col_block), (slots * row_block, PB)
        ).reshape(slots, row_block, PB)
        heads.append(jnp.stack([part[orders[h].index(s)] for s in range(slots)]))
    head_rows = jnp.where(par_index < par_size // 2, heads[0], heads[1])
    sides = [head_rows[:, :, : PB // 2], head_rows[:, :, PB // 2 :]]
    sides = [jnp.stack([sides[h][s] for s in orders[h]]) for h in range(2)]
    for step in range(chip_bits):
        mid = sides[0].shape[0] // 2
        moved = [permute(sides[h][mid:], "walk", walk_size, 2 << sweeps[h][step]) for h in range(2)]
        sides = [sides[h][:mid] + moved[h] for h in range(2)]
    rows_mine = jnp.concatenate([sides[0][0], sides[1][0]], axis=1)
    bit = par_size // 2
    while bit:
        rows_mine = rows_mine + permute(rows_mine, "par", par_size, bit)
        bit //= 2
    all_rows = rows_mine[None]
    for bit in [2 << b for b in range(chip_bits)] + [1]:
        all_rows = jnp.concatenate([all_rows, permute(all_rows, "walk", walk_size, bit)], axis=0)
    flips = [0]
    for bit in [2 << b for b in range(chip_bits)] + [1]:
        flips += [f | bit for f in flips]
    where_flip = np.argsort(np.array(flips))

    def rows_of(block_index):
        at = jnp.asarray(where_flip)[block_index ^ walk_index]
        return lax.dynamic_index_in_dim(all_rows, at, 0, keepdims=False)

    def shift_at(first_row, count):
        ids = first_row + jnp.arange(count, dtype=jnp.int32)
        return SHIFT * (ids[:, None] == jnp.arange(PB, dtype=jnp.int32)[None, :]).astype(jnp.float32)

    head = jnp.concatenate([rows_of(b) for b in range(-(-PB // row_block))], axis=0)[:PB]
    inverse = head_inverse(head + shift_at(0, PB))
    own_panel = outer_rows(rows_mine + shift_at(walk_index * row_block, row_block), inverse)
    per_col = col_block // row_block
    col_rows = jnp.concatenate([rows_of(par_index * per_col + b) for b in range(per_col)], axis=0)
    col_panel = outer_rows(col_rows + shift_at(par_index * col_block, col_block), inverse)

    for step in range(chip_bits):
        moved = []
        for h in range(2):
            mid = halves[h].shape[0] // 2
            bit = 2 << sweeps[h][step]
            moved.append(permute(halves[h][mid:], "walk", walk_size, bit))
        halves = [halves[h][: halves[h].shape[0] // 2] + moved[h] for h in range(2)]
    gram = halves[0] + permute(halves[1], "par", par_size, par_size // 2)
    bit = par_size // 4
    while bit:
        mid = gram.shape[1] // 2
        gram = gram[:, :mid] + permute(gram[:, mid:], "par", par_size, bit)
        bit //= 2
    row_ids = walk_index * row_block + jnp.arange(row_block, dtype=jnp.int32)
    col_ids = par_index * col_block + jnp.arange(col_block, dtype=jnp.int32)
    shifted = gram + SHIFT * (row_ids[:, None] == col_ids[None, :]).astype(jnp.float32)
    trailing = shifted - outer_rows(own_panel, col_panel)
    return (own_panel, trailing)


def solution(mesh):
    in_specs = (P(("walk", "par"), None, None), P(("walk", "par"), None, None), P(), P(), P())
    out_specs = (P("walk", None), P("walk", "par"))
    return jax.shard_map(
        on_device, mesh=mesh, in_specs=in_specs, out_specs=out_specs, check_vma=False
    )
```

```python
import functools
import math

import jax
import jax.numpy as jnp
import numpy as np
from jax import lax
from jax.experimental import pallas as pl
from jax.experimental.pallas import tpu as pltpu
from jax.sharding import PartitionSpec as P

PB = 256
HIGHEST = lax.Precision.HIGHEST
SHIFT = 0.05
LANES = 256
SUB = 8
CONTRACT_LAST = (((1,), (1,)), ((), ()))
VMEM_LIMIT = 60 * 1024 * 1024


def outer_rows(left_rows, right_rows):
    return lax.dot_general(left_rows, right_rows, CONTRACT_LAST, precision=HIGHEST)


def xor_pairs(size, bit):
    return [(i, i ^ bit) for i in range(size)]


class Plan:
    def __init__(self, walk_size, par_size):
        self.walk_size, self.par_size = walk_size, par_size
        par_bits = par_size.bit_length() - 1
        walk_bits = walk_size.bit_length() - 1
        self.dims = []
        for bit in reversed(range(par_bits)):
            self.dims.append(("par", 1 << bit, "J" if bit == 0 else "I"))
        for bit in range(1, walk_bits):
            self.dims.append(("walk", 1 << bit, "J" if bit == walk_bits - 1 else "I"))
        self.place = []
        seen = {"I": 0, "J": 0}
        for _, _, kind in self.dims:
            self.place.append(seen[kind])
            seen[kind] += 1
        self.blocks = {"F": 1 << seen["I"], "S": 1 << seen["J"]}
        self.order = {
            side: sorted(
                range(len(self.dims)), key=lambda k: (self.dims[k][0] == "walk", not self.splits(side, self.dims[k][2]))
            )
            for side in ("F", "S")
        }
        self.rounds = self.schedule()

    def splits(self, side, kind):
        return (side == "F") == (kind == "I")

    def depth(self, side, src, rb, after):
        best = 0
        order = self.order[side]
        for k in order[order.index(after) + 1 :]:
            if self.splits(side, self.dims[k][2]):
                if rb >> self.place[k] & 1:
                    return max(best, 1 + self.depth(side, src, rb ^ (1 << self.place[k]), k))
            else:
                best = max(best, 1 + self.depth(side, src, rb, k))
        return best

    def tasks(self):
        out = []
        for side in ("F", "S"):
            live = [(0, rb) for rb in range(self.blocks[side])]
            for k in self.order[side]:
                kind = self.dims[k][2]
                kept, made = [], []
                for src, rb in live:
                    if self.splits(side, kind):
                        p = self.place[k]
                        if rb >> p & 1:
                            made.append((k, (side, src, rb), (side, src | 1 << k, rb ^ (1 << p))))
                        else:
                            kept.append((src, rb))
                    else:
                        kept.append((src, rb))
                        made.append((k, (side, src, rb), (side, src | 1 << k, rb)))
                live = kept + [dst[1:] for _, _, dst in made]
                out += made
        return out

    def schedule(self):
        left = self.tasks()
        have = {(side, 0, rb) for side in ("F", "S") for rb in range(self.blocks[side])}
        rounds = []
        while left:
            chosen = []
            for k, (axis, _, _) in enumerate(self.dims):
                ready = [t for t in left if t[0] == k and t[1] in have]
                ready.sort(
                    key=lambda t: (
                        not self.splits(t[1][0], self.dims[k][2]),
                        axis == "par" and (t[2][1] & (self.par_size - 1)).bit_count(),
                        -self.depth(*t[2], k),
                    )
                )
                chosen += ready[: 1 if axis == "par" else 2]
            left = [t for t in left if t not in chosen]
            have |= {t[2] for t in chosen}
            rounds.append(chosen)
        return rounds

    def flip(self, src):
        walk = par = 0
        for k, (axis, bit, _) in enumerate(self.dims):
            if src >> k & 1:
                walk, par = (walk | bit, par) if axis == "walk" else (walk, par | bit)
        return walk, par


def permute(value, axis, size, bit):
    return lax.ppermute(value, axis, xor_pairs(size, bit))


def exchange(plan, pieces, block):
    sizes = {"walk": plan.walk_size, "par": plan.par_size}
    held = dict(pieces)
    planes, chips = plan.par_size, plan.walk_size // 2
    members = {q: [q | m * planes for m in range(chips)] for q in range(planes)}
    waiting = list(range(planes))
    own, other, sent = {}, {}, []
    gate = []
    rounds = list(plan.rounds)
    while rounds or waiting or sent:
        chosen = rounds.pop(0) if rounds else []
        groups = {}
        for k, src, dst in chosen:
            groups.setdefault((k, held[src].shape), []).append((src, dst))
        keys = sorted({s for pairs in groups.values() for s, _ in pairs})
        if keys and (gate or sent):
            tied = lax.optimization_barrier(
                tuple(held[n] for n in keys) + tuple(held[n] for n in gate) + tuple(own[q] for q in sent)
            )
            for n, v in zip(keys + gate, tied):
                held[n] = v
            for q, v in zip(sent, tied[len(keys) + len(gate) :]):
                own[q] = v
        gate = []
        for q in sent:
            other[q] = permute(own[q], "walk", plan.walk_size, 1)
        sent = []
        for q in list(waiting):
            if all((side, m, 0) in held for side in ("F", "S") for m in members[q]):
                own[q] = block([held["F", m, 0] for m in members[q]], [held["S", m, 0] for m in members[q]])
                waiting.remove(q)
                sent.append(q)
        for (k, _), pairs in groups.items():
            axis, bit, _ = plan.dims[k]
            if len(pairs) == 1:
                held[pairs[0][1]] = permute(held[pairs[0][0]], axis, sizes[axis], bit)
            else:
                moved = permute(jnp.stack([held[s] for s, _ in pairs]), axis, sizes[axis], bit)
                for i, (_, d) in enumerate(pairs):
                    held[d] = moved[i]
            gate += [d for _, d in pairs]
    return [own[q] for q in range(planes)] + [other[q] for q in range(planes)], [
        [(m, core) for m in members[q]] for core in range(2) for q in range(planes)
    ]


def turned_kernel(counts, own, live_ref, f_ref, s_ref, *refs):
    outs, turned_ref = refs[:-1], refs[-1]
    done = 0
    for side, (ref, count) in enumerate(zip((f_ref, s_ref), counts)):
        turned = ref[...].astype(jnp.float32).T
        turned_ref[...] = jnp.where(live_ref[...] > 0, turned, 0.0) if side == 0 else turned
        size = turned.shape[0] // count
        for rb in range(count):
            at = pl.multiple_of((own[side] ^ rb) * size, SUB)
            outs[done + rb][...] = turned_ref[pl.ds(at, size), :]
        done += count


def turned_pieces(own, live, features, signals, counts):
    rows, width = features.shape
    whole = pl.BlockSpec(memory_space=pltpu.VMEM)
    shapes = [jax.ShapeDtypeStruct((width // n, rows), jnp.float32) for n in counts for _ in range(n)]
    return pl.pallas_call(
        functools.partial(turned_kernel, counts),
        out_shape=shapes,
        in_specs=[pl.BlockSpec(memory_space=pltpu.SMEM), whole, whole, whole],
        out_specs=[whole] * len(shapes),
        scratch_shapes=[pltpu.VMEM((width, rows), jnp.float32)],
        compiler_params=pltpu.CompilerParams(vmem_limit_bytes=VMEM_LIMIT),
        name="turned_pieces",
    )(own, live, features, signals)


def jacobian_kernel(slots, count, *refs):
    lefts, rights, scale_ref, out_ref = refs[:count], refs[count : 2 * count], refs[2 * count], refs[-1]
    ib = lefts[0].shape[0]
    jb = rights[0].shape[0]
    together = LANES // slots
    parts = LANES // jb
    lane = lax.broadcasted_iota(jnp.int32, (together, LANES), 1)
    row = lax.broadcasted_iota(jnp.int32, (together, LANES), 0)
    mine = (lane >= row * slots) & (lane < row * slots + slots)
    for n in range(count):
        left = lefts[n][...]
        right = rights[n][...].astype(jnp.bfloat16)
        spread = jnp.where(mine[None], left[:, None, :], 0.0).reshape(ib * together, LANES)
        block = lax.dot_general(
            spread.astype(jnp.bfloat16), right, CONTRACT_LAST, preferred_element_type=jnp.float32
        )
        block = block.reshape(parts, ib // parts, together, jb)
        for b in range(parts):
            out_ref[:, n, :, b * jb : (b + 1) * jb] = block[b] * scale_ref[:, b * jb : (b + 1) * jb][:, None, :]


def jacobian(lefts, rights, scaling, slots):
    count = len(lefts)
    ib, lanes = lefts[0].shape
    jb = rights[0].shape[0]
    tiles = ib * jb // LANES
    together = LANES // slots
    return pl.pallas_call(
        functools.partial(jacobian_kernel, slots, count),
        out_shape=jax.ShapeDtypeStruct((tiles, count, lanes // slots, LANES), jnp.float32),
        grid=(lanes // LANES,),
        in_specs=[pl.BlockSpec((ib, LANES), lambda g: (0, g))] * count
        + [pl.BlockSpec((jb, LANES), lambda g: (0, g))] * count
        + [pl.BlockSpec((tiles, LANES), lambda g: (0, 0))],
        out_specs=pl.BlockSpec((tiles, count, together, LANES), lambda g: (0, 0, g, 0)),
        compiler_params=pltpu.CompilerParams(vmem_limit_bytes=VMEM_LIMIT),
        name="jacobian",
    )(*lefts, *rights, scaling)


def split_two(value):
    high = value.astype(jnp.bfloat16)
    return high, (value - high.astype(jnp.float32)).astype(jnp.bfloat16)


def product_rows(high_ref, low_ref, at, size, swap):
    at = pl.ds(at if isinstance(at, int) else pl.multiple_of(at, 16), size)
    h, l = high_ref[0, at, :], low_ref[0, at, :]
    return jnp.concatenate([h, l, h] if swap else [h, h, l], axis=1)


def centre_kernel(row_block, col_block, orders, count, row_at, col_at, place_at, *refs):
    pieces = refs[:count]
    hot_ref, hot_t_ref, recip_ref = refs[count : count + 3]
    far_a, far_b, near_a, near_b, value_ref, high_ref, low_ref = refs[count + 3 :]

    @pl.when(pl.program_id(0) == 0)
    def _():
        for ref in (far_a, far_b, near_a, near_b):
            ref[...] = jnp.zeros_like(ref)

    members, rows = pieces[0].shape[1:3]
    for a in range(count):
        for m in range(members):
            value_ref[pl.ds(pl.multiple_of(place_at[a * members + m], 8), rows), :] = pieces[a][0, m]
    value = value_ref[...]
    high, low = split_two(value)
    dot = functools.partial(jnp.dot, preferred_element_type=jnp.float32)
    means = (dot(hot_t_ref[...], high) + dot(hot_t_ref[...], low)) * recip_ref[...]
    first, second = split_two(means)
    hot = hot_ref[...]
    high_ref[0], low_ref[0] = split_two(value - (dot(hot, first) + dot(hot, second)))

    blocks = col_at.shape[0]
    width = blocks // 4 * col_block
    for h, (far, near) in enumerate(((far_a, near_a), (far_b, near_b))):
        left = jnp.concatenate(
            [product_rows(high_ref, low_ref, row_at[s], row_block, False) for s in orders[h]], axis=0
        )
        near_cols = list(range(h * blocks // 4, (h + 1) * blocks // 4))
        far_cols = [n + blocks // 2 for n in near_cols]
        right = jnp.concatenate(
            [product_rows(high_ref, low_ref, col_at[n], col_block, True) for n in near_cols + far_cols], axis=0
        )
        got = lax.dot_general(left, right, CONTRACT_LAST, preferred_element_type=jnp.float32)
        near[...] += got[:, :width]
        far[...] += got[:, width:]


def gram_rows(pieces, hot, hot_t, recip, row_at, col_at, place_at, row_block, col_block, orders):
    tiles, members, rows, lanes = pieces[0].shape
    walkers, groups = hot.shape
    slots = len(orders[0])
    quarter = jax.ShapeDtypeStruct((slots * row_block, walkers // 4), jnp.float32)
    fixed = lambda t, *_: (0, 0)
    parts = pl.pallas_call(
        functools.partial(centre_kernel, row_block, col_block, orders, len(pieces)),
        out_shape=(quarter,) * 4,
        grid_spec=pltpu.PrefetchScalarGridSpec(
            num_scalar_prefetch=3,
            grid=(tiles,),
            in_specs=[pl.BlockSpec((1, members, rows, lanes), lambda t, *_: (t, 0, 0, 0))] * len(pieces)
            + [
                pl.BlockSpec((walkers, groups), fixed),
                pl.BlockSpec((groups, walkers), fixed),
                pl.BlockSpec((groups, 1), fixed),
            ],
            out_specs=(pl.BlockSpec(quarter.shape, fixed),) * 4,
            scratch_shapes=[
                pltpu.VMEM((walkers, lanes), jnp.float32),
                pltpu.VMEM((1, walkers, lanes), jnp.bfloat16),
                pltpu.VMEM((1, walkers, lanes), jnp.bfloat16),
            ],
        ),
        compiler_params=pltpu.CompilerParams(vmem_limit_bytes=VMEM_LIMIT),
        name="gram_rows",
    )(row_at, col_at, place_at, *pieces, hot, hot_t, recip)
    return parts[:2], parts[2:]


def inverse_factor(value):
    size = value.shape[0]
    lane = lax.broadcasted_iota(jnp.int32, (1, size), 1)
    sub = lax.broadcasted_iota(jnp.int32, (SUB, 1), 0)
    tiles = [value[t * SUB : (t + 1) * SUB] for t in range(size // SUB)]
    for j in range(size):
        home, at = divmod(j, SUB)
        row = tiles[home][at : at + 1]
        scaled = jnp.where(lane == j, 1.0, row) / row[:, j : j + 1]
        for t in range(home, len(tiles)):
            tile = tiles[t]
            factor = tile[:, j : j + 1]
            clear = lane == j
            if t == home:
                if at == SUB - 1:
                    continue
                factor = jnp.where(sub > at, factor, 0.0)
                clear = clear & (sub > at)
            tiles[t] = jnp.where(clear, 0.0, tile) - factor * scaled
    value = jnp.concatenate(tiles, axis=0)
    row_id = lax.broadcasted_iota(jnp.int32, (size, 1), 0)
    diagonal = jnp.sum(jnp.where(lane == row_id, value, 0.0), axis=1, keepdims=True)
    unit = jnp.where(lane < row_id, value, jnp.where(lane == row_id, 1.0, 0.0))
    return unit / jnp.sqrt(diagonal)


def head_kernel(a_ref, out_ref, work_ref, below_ref):
    half = work_ref.shape[0]
    dot = functools.partial(lax.dot_general, precision=HIGHEST, preferred_element_type=jnp.float32)
    first = pl.program_id(0) == 0
    @pl.when(first)
    def _():
        work_ref[...] = a_ref[:half, :half]
    inverse = inverse_factor(work_ref[...])
    @pl.when(first)
    def _():
        out_ref[:half, :half] = inverse
        out_ref[:half, half:] = jnp.zeros((half, half), jnp.float32)
        below = dot(a_ref[half:, :half], inverse, CONTRACT_LAST)
        below_ref[...] = below
        work_ref[...] = a_ref[half:, half:] - dot(below, below, CONTRACT_LAST)
    @pl.when(jnp.logical_not(first))
    def _():
        out_ref[half:, half:] = inverse
        plain = (((1,), (0,)), ((), ()))
        out_ref[half:, :half] = -dot(inverse, dot(below_ref[...], out_ref[:half, :half], plain), plain)


def head_inverse(head):
    size = head.shape[0]
    fixed = pl.BlockSpec((size, size), lambda i: (0, 0))
    return pl.pallas_call(
        head_kernel,
        out_shape=jax.ShapeDtypeStruct(head.shape, jnp.float32),
        grid=(2,),
        in_specs=[fixed],
        out_specs=fixed,
        scratch_shapes=[pltpu.VMEM((size // 2, size // 2), jnp.float32)] * 2,
        name="head_inverse",
    )(head)


def on_device(features, signals, param_scale, geometry, electrons):
    par_size = lax.axis_size("par")
    walk_size = lax.axis_size("walk")
    walk_index = lax.axis_index("walk")
    par_index = lax.axis_index("par")
    per_device, slots_count, width = features.shape
    walkers = geometry.shape[0]
    groups = electrons.shape[0]
    row_block = per_device * par_size
    col_block = walkers // par_size
    plan = Plan(walk_size, par_size)

    anchor = (walk_index * par_size + par_index) * per_device
    own_geometry = lax.dynamic_slice_in_dim(geometry, anchor, per_device)
    own_matches = own_geometry[:, None] == jnp.arange(groups, dtype=jnp.int32)[None, :]
    own_electrons = jnp.sum(jnp.where(own_matches, electrons[None, :], 0), axis=1)
    live = (jnp.arange(slots_count, dtype=jnp.int32)[None, :] < own_electrons[:, None]).astype(jnp.float32)

    own = {"F": 0, "S": 0}
    for k, (axis, bit, kind) in enumerate(plan.dims):
        index = walk_index if axis == "walk" else par_index
        side = "F" if kind == "I" else "S"
        own[side] = own[side] + jnp.where((index & bit) != 0, 1 << plan.place[k], 0)
    flat = per_device * slots_count
    counts = (plan.blocks["F"], plan.blocks["S"])
    turned = turned_pieces(
        jnp.stack([own["F"], own["S"]]).astype(jnp.int32),
        live.reshape(1, flat),
        features.reshape(flat, width),
        signals.reshape(flat, width),
        counts,
    )
    names = [("F", 0, rb) for rb in range(counts[0])] + [("S", 0, rb) for rb in range(counts[1])]
    pieces = dict(zip(names, turned))
    ib, jb = width // plan.blocks["F"], width // plan.blocks["S"]
    parts = LANES // jb
    scaling = param_scale * (1.0 / math.sqrt(slots_count * width * width))
    scaling = lax.dynamic_slice(scaling, (own["F"] * ib, own["S"] * jb), (ib, jb))
    scaling = scaling.reshape(parts, ib // parts, jb).transpose(1, 0, 2).reshape(ib // parts, LANES)
    columns, names = exchange(plan, pieces, lambda f, s: jacobian(f, s, scaling, slots_count))
    place_at = []
    for src, core in [n for members in names for n in members]:
        walk_flip, par_flip = plan.flip(src)
        place_at.append((walk_index ^ (walk_flip | core)) * par_size + (par_index ^ par_flip))
    place_at = (jnp.stack(place_at) * per_device).astype(jnp.int32)

    matches = geometry[:, None] == jnp.arange(groups, dtype=jnp.int32)[None, :]
    hot = matches.astype(jnp.bfloat16)
    hot_t = (jnp.arange(groups, dtype=jnp.int32)[:, None] == geometry[None, :]).astype(jnp.bfloat16)
    counts = jnp.maximum(jnp.sum(matches.astype(jnp.float32), axis=0), 1.0)
    recip = (1.0 / counts)[:, None]

    chip_bits = walk_size.bit_length() - 2
    slots = 1 << chip_bits
    core, chip = walk_index & 1, walk_index >> 1
    row_at = jnp.stack([((chip ^ s) * 2 + core) * row_block for s in range(slots)]).astype(jnp.int32)
    col_at = jnp.stack([(par_index ^ p) * col_block for p in range(par_size)]).astype(jnp.int32)
    up = list(range(chip_bits))
    sweeps = (up, up[::-1])
    orders = tuple(
        tuple(sorted(range(slots), key=lambda s, o=o: [s >> b & 1 for b in o])) for o in sweeps
    )
    far, near = gram_rows(
        columns, hot, hot_t, recip, row_at, col_at, place_at, row_block, col_block, orders
    )

    def after(values, *others):
        tied = lax.optimization_barrier(tuple(values) + others)
        return list(tied[: len(values)])

    def plane_step(pair, step):
        mid = pair[0].shape[0] // 2
        return [permute(pair[h][mid:], "walk", walk_size, 2 << sweeps[h][step]) for h in range(2)]

    def plane_add(pair, moved):
        return [pair[h][: pair[h].shape[0] // 2] + moved[h] for h in range(2)]

    far, near = list(far), list(near)
    each = max(par_size // 4, 1)
    at = (par_index % each) * col_block
    head_cols = []
    for h in range(2):
        picked = None
        for q, part in enumerate(near + far):
            cols = lax.dynamic_slice(part, (0, at + h * PB // 2), (slots * row_block, PB // 2))
            if q % 2 != h:
                cols = cols.reshape(slots, row_block, PB // 2)
                cols = jnp.concatenate([cols[orders[q % 2].index(s)] for s in orders[h]], axis=0)
            picked = cols if picked is None else jnp.where(par_index // each == q, cols, picked)
        head_cols.append(picked)

    head_cols = plane_add(head_cols, plane_step(head_cols, 0))
    tied = after([*head_cols, *far, *near])
    head_cols, far, near = tied[:2], tied[2:4], tied[4:]
    far_moved = plane_step(far, 0)
    for step in range(1, chip_bits):
        head_cols = plane_add(head_cols, plane_step(head_cols, step))
    rows_mine = jnp.concatenate(head_cols, axis=1)
    bit = par_size // 2
    rows_mine = rows_mine + permute(rows_mine, "par", par_size, bit)
    far = plane_add(far, far_moved)
    rows_mine, far[0], far[1] = after([rows_mine, *far])
    for step in range(1, chip_bits):
        far_moved = plane_step(far, step)
        if step < chip_bits - 1:
            far = plane_add(far, far_moved)
    bit //= 2
    while bit:
        rows_mine = rows_mine + permute(rows_mine, "par", par_size, bit)
        bit //= 2

    chips = walk_size // 2
    per_col = col_block // row_block
    top_count = -(-PB // row_block)

    def spread(holder):
        total = jnp.where(chip == jnp.asarray([holder(z) for z in range(par_size)])[par_index], rows_mine, 0.0)
        for flip in range(1, chips):
            pairs = []
            for z in range(par_size):
                for c in range(2):
                    pairs.append(
                        ((holder(z) * 2 + c) * par_size + z, ((holder(z) ^ flip) * 2 + c) * par_size + z)
                    )
            total = total + lax.ppermute(rows_mine, ("walk", "par"), pairs)
        return total

    both = jnp.stack([spread(lambda z: 0), spread(lambda z: z)])
    far = plane_add(far, far_moved)
    both, far[0], far[1] = after([both, *far])
    far = [permute(part, "par", par_size, par_size // 2) for part in far]
    near_moved = plane_step(near, 0)
    swapped = permute(both, "walk", walk_size, 1)
    near = plane_add(near, near_moved)
    swapped, near[0], near[1] = after([swapped, *near])
    for step in range(1, chip_bits):
        near = plane_add(near, plane_step(near, step))
    pair = [jnp.where(core == 0, both, swapped), jnp.where(core == 0, swapped, both)]
    head = jnp.concatenate([pair[0][0], pair[1][0]], axis=0)[:PB]
    col_rows = jnp.concatenate([pair[0][1], pair[1][1]], axis=0)

    def shift_at(first_row, count):
        ids = first_row + jnp.arange(count, dtype=jnp.int32)
        return SHIFT * (ids[:, None] == jnp.arange(PB, dtype=jnp.int32)[None, :]).astype(jnp.float32)

    inverse = head_inverse(head + shift_at(0, PB))
    near = [part + got for part, got in zip(near, far)]
    moved = permute(near[1], "par", par_size, par_size // 4)
    inverse, near[0], near[1] = after([inverse, *near])
    own_panel = outer_rows(rows_mine + shift_at(walk_index * row_block, row_block), inverse)
    col_panel = outer_rows(col_rows + shift_at(par_index * col_block, col_block), inverse)
    update = outer_rows(own_panel, col_panel)
    gram = near[0] + moved
    bit = par_size // 8
    while bit:
        mid = gram.shape[1] // 2
        gram = gram[:, :mid] + permute(gram[:, mid:], "par", par_size, bit)
        bit //= 2
    row_ids = walk_index * row_block + jnp.arange(row_block, dtype=jnp.int32)
    col_ids = par_index * col_block + jnp.arange(col_block, dtype=jnp.int32)
    shifted = gram + SHIFT * (row_ids[:, None] == col_ids[None, :]).astype(jnp.float32)
    return (own_panel, shifted - update)


def solution(mesh):
    in_specs = (P(("walk", "par"), None, None), P(("walk", "par"), None, None), P(), P(), P())
    out_specs = (P("walk", None), P("walk", "par"))
    return jax.shard_map(
        on_device, mesh=mesh, in_specs=in_specs, out_specs=out_specs, check_vma=False
    )
```

```python
import functools
import math

import jax
import jax.numpy as jnp
import numpy as np
from jax import lax
from jax.experimental import pallas as pl
from jax.experimental.pallas import tpu as pltpu
from jax.sharding import PartitionSpec as P

PB = 256
HIGHEST = lax.Precision.HIGHEST
SHIFT = 0.05
LANES = 256
SUB = 8
TOGETHER = 2
CONTRACT_LAST = (((1,), (1,)), ((), ()))
VMEM_LIMIT = 60 * 1024 * 1024


def outer_rows(left_rows, right_rows):
    return lax.dot_general(left_rows, right_rows, CONTRACT_LAST, precision=HIGHEST)


def xor_pairs(size, bit):
    return [(i, i ^ bit) for i in range(size)]


class Plan:
    def __init__(self, walk_size, par_size):
        self.walk_size, self.par_size = walk_size, par_size
        par_bits = par_size.bit_length() - 1
        walk_bits = walk_size.bit_length() - 1
        self.dims = []
        for bit in reversed(range(par_bits)):
            self.dims.append(("par", 1 << bit, "J" if bit == 0 else "I"))
        for bit in range(1, walk_bits):
            self.dims.append(("walk", 1 << bit, "J" if bit == walk_bits - 1 else "I"))
        self.place = []
        seen = {"I": 0, "J": 0}
        for _, _, kind in self.dims:
            self.place.append(seen[kind])
            seen[kind] += 1
        self.blocks = {"F": 1 << seen["I"], "S": 1 << seen["J"]}
        self.order = {
            side: sorted(
                range(len(self.dims)), key=lambda k: (self.dims[k][0] == "walk", not self.splits(side, self.dims[k][2]))
            )
            for side in ("F", "S")
        }
        self.rounds = self.schedule()

    def splits(self, side, kind):
        return (side == "F") == (kind == "I")

    def depth(self, side, src, rb, after):
        best = 0
        order = self.order[side]
        for k in order[order.index(after) + 1 :]:
            if self.splits(side, self.dims[k][2]):
                if rb >> self.place[k] & 1:
                    return max(best, 1 + self.depth(side, src, rb ^ (1 << self.place[k]), k))
            else:
                best = max(best, 1 + self.depth(side, src, rb, k))
        return best

    def tasks(self):
        out = []
        for side in ("F", "S"):
            live = [(0, rb) for rb in range(self.blocks[side])]
            for k in self.order[side]:
                kind = self.dims[k][2]
                kept, made = [], []
                for src, rb in live:
                    if self.splits(side, kind):
                        p = self.place[k]
                        if rb >> p & 1:
                            made.append((k, (side, src, rb), (side, src | 1 << k, rb ^ (1 << p))))
                        else:
                            kept.append((src, rb))
                    else:
                        kept.append((src, rb))
                        made.append((k, (side, src, rb), (side, src | 1 << k, rb)))
                live = kept + [dst[1:] for _, _, dst in made]
                out += made
        return out

    def schedule(self):
        left = self.tasks()
        have = {(side, 0, rb) for side in ("F", "S") for rb in range(self.blocks[side])}
        rounds = []
        while left:
            chosen = []
            for k, (axis, _, _) in enumerate(self.dims):
                ready = [t for t in left if t[0] == k and t[1] in have]
                ready.sort(
                    key=lambda t: (
                        not self.splits(t[1][0], self.dims[k][2]),
                        axis == "par" and (t[2][1] & (self.par_size - 1)).bit_count(),
                        -self.depth(*t[2], k),
                    )
                )
                chosen += ready[: 1 if axis == "par" else 2]
            left = [t for t in left if t not in chosen]
            have |= {t[2] for t in chosen}
            rounds.append(chosen)
        return rounds

    def flip(self, src):
        walk = par = 0
        for k, (axis, bit, _) in enumerate(self.dims):
            if src >> k & 1:
                walk, par = (walk | bit, par) if axis == "walk" else (walk, par | bit)
        return walk, par


def permute(value, axis, size, bit):
    return lax.ppermute(value, axis, xor_pairs(size, bit))


def exchange(plan, pieces, block):
    sizes = {"walk": plan.walk_size, "par": plan.par_size}
    held = dict(pieces)
    planes, chips = plan.par_size, plan.walk_size // 2
    members = {q: [q | m * planes for m in range(chips)] for q in range(planes)}
    waiting = list(range(planes))
    own, other, sent = {}, {}, []
    gate = []
    rounds = list(plan.rounds)
    while rounds or waiting or sent:
        chosen = rounds.pop(0) if rounds else []
        groups = {}
        for k, src, dst in chosen:
            groups.setdefault((k, held[src].shape), []).append((src, dst))
        keys = sorted({s for pairs in groups.values() for s, _ in pairs})
        if keys and (gate or sent):
            tied = lax.optimization_barrier(
                tuple(held[n] for n in keys) + tuple(held[n] for n in gate) + tuple(own[q] for q in sent)
            )
            for n, v in zip(keys + gate, tied):
                held[n] = v
            for q, v in zip(sent, tied[len(keys) + len(gate) :]):
                own[q] = v
        gate = []
        for q in sent:
            other[q] = permute(own[q], "walk", plan.walk_size, 1)
        sent = []
        for q in list(waiting):
            if all((side, m, 0) in held for side in ("F", "S") for m in members[q]):
                own[q] = block([held["F", m, 0] for m in members[q]], [held["S", m, 0] for m in members[q]])
                waiting.remove(q)
                sent.append(q)
        for (k, _), pairs in groups.items():
            axis, bit, _ = plan.dims[k]
            if len(pairs) == 1:
                held[pairs[0][1]] = permute(held[pairs[0][0]], axis, sizes[axis], bit)
            else:
                moved = permute(jnp.stack([held[s] for s, _ in pairs]), axis, sizes[axis], bit)
                for i, (_, d) in enumerate(pairs):
                    held[d] = moved[i]
            gate += [d for _, d in pairs]
    return [own[q] for q in range(planes)] + [other[q] for q in range(planes)], [
        [(m, core) for m in members[q]] for core in range(2) for q in range(planes)
    ]


def turned_kernel(counts, own, live_ref, f_ref, s_ref, *refs):
    outs, turned_ref = refs[:-1], refs[-1]
    done = 0
    for side, (ref, count) in enumerate(zip((f_ref, s_ref), counts)):
        turned = ref[...].astype(jnp.float32).T
        turned_ref[...] = jnp.where(live_ref[...] > 0, turned, 0.0) if side == 0 else turned
        size = turned.shape[0] // count
        for rb in range(count):
            at = pl.multiple_of((own[side] ^ rb) * size, SUB)
            outs[done + rb][...] = turned_ref[pl.ds(at, size), :]
        done += count


def turned_pieces(own, live, features, signals, counts):
    rows, width = features.shape
    whole = pl.BlockSpec(memory_space=pltpu.VMEM)
    shapes = [jax.ShapeDtypeStruct((width // n, rows), jnp.float32) for n in counts for _ in range(n)]
    return pl.pallas_call(
        functools.partial(turned_kernel, counts),
        out_shape=shapes,
        in_specs=[pl.BlockSpec(memory_space=pltpu.SMEM), whole, whole, whole],
        out_specs=[whole] * len(shapes),
        scratch_shapes=[pltpu.VMEM((width, rows), jnp.float32)],
        compiler_params=pltpu.CompilerParams(vmem_limit_bytes=VMEM_LIMIT),
        name="turned_pieces",
    )(own, live, features, signals)


def jacobian_kernel(slots, count, *refs):
    lefts, rights, scale_ref, out_ref = refs[:count], refs[count : 2 * count], refs[2 * count], refs[-1]
    ib = lefts[0].shape[0]
    jb = rights[0].shape[0]
    together = LANES // slots
    parts = LANES // jb
    lane = lax.broadcasted_iota(jnp.int32, (together, LANES), 1)
    row = lax.broadcasted_iota(jnp.int32, (together, LANES), 0)
    mine = (lane >= row * slots) & (lane < row * slots + slots)
    for n in range(count):
        left = lefts[n][...]
        right = rights[n][...].astype(jnp.bfloat16)
        spread = jnp.where(mine[None], left[:, None, :], 0.0).reshape(ib * together, LANES)
        block = lax.dot_general(
            spread.astype(jnp.bfloat16), right, CONTRACT_LAST, preferred_element_type=jnp.float32
        )
        block = block.reshape(parts, ib // parts, together, jb)
        for b in range(parts):
            out_ref[:, n, :, b * jb : (b + 1) * jb] = block[b] * scale_ref[:, b * jb : (b + 1) * jb][:, None, :]


def jacobian(lefts, rights, scaling, slots):
    count = len(lefts)
    ib, lanes = lefts[0].shape
    jb = rights[0].shape[0]
    tiles = ib * jb // LANES
    together = LANES // slots
    return pl.pallas_call(
        functools.partial(jacobian_kernel, slots, count),
        out_shape=jax.ShapeDtypeStruct((tiles, count, lanes // slots, LANES), jnp.float32),
        grid=(lanes // LANES,),
        in_specs=[pl.BlockSpec((ib, LANES), lambda g: (0, g))] * count
        + [pl.BlockSpec((jb, LANES), lambda g: (0, g))] * count
        + [pl.BlockSpec((tiles, LANES), lambda g: (0, 0))],
        out_specs=pl.BlockSpec((tiles, count, together, LANES), lambda g: (0, 0, g, 0)),
        compiler_params=pltpu.CompilerParams(vmem_limit_bytes=VMEM_LIMIT),
        name="jacobian",
    )(*lefts, *rights, scaling)


def split_two(value):
    high = value.astype(jnp.bfloat16)
    return high, (value - high.astype(jnp.float32)).astype(jnp.bfloat16)


def product_rows(high_ref, low_ref, at, size, swap):
    at = pl.ds(at if isinstance(at, int) else pl.multiple_of(at, 16), size)
    parts = []
    for i in range(high_ref.shape[0]):
        h, l = high_ref[i, at, :], low_ref[i, at, :]
        parts += [h, l, h] if swap else [h, h, l]
    return jnp.concatenate(parts, axis=1)


def centre_kernel(row_block, col_block, orders, count, row_at, col_at, place_at, *refs):
    pieces = refs[:count]
    hot_ref, hot_t_ref, recip_ref = refs[count : count + 3]
    far_a, far_b, near_a, near_b, value_ref, high_ref, low_ref = refs[count + 3 :]

    @pl.when(pl.program_id(0) == 0)
    def _():
        for ref in (far_a, far_b, near_a, near_b):
            ref[...] = jnp.zeros_like(ref)

    members, rows = pieces[0].shape[1:3]
    dot = functools.partial(jnp.dot, preferred_element_type=jnp.float32)
    for i in range(high_ref.shape[0]):
        for a in range(count):
            for m in range(members):
                at = pl.multiple_of(place_at[a * members + m], 8)
                value_ref[i, pl.ds(at, rows), :] = pieces[a][i, m]
        value = value_ref[i]
        high, low = split_two(value)
        means = (dot(hot_t_ref[...], high) + dot(hot_t_ref[...], low)) * recip_ref[...]
        means = jnp.concatenate(split_two(means), axis=0)
        high_ref[i], low_ref[i] = split_two(value - dot(hot_ref[...], means))

    blocks = col_at.shape[0]
    width = blocks // 4 * col_block
    for h, (far, near) in enumerate(((far_a, near_a), (far_b, near_b))):
        left = jnp.concatenate(
            [product_rows(high_ref, low_ref, row_at[s], row_block, False) for s in orders[h]], axis=0
        )
        near_cols = list(range(h * blocks // 4, (h + 1) * blocks // 4))
        far_cols = [n + blocks // 2 for n in near_cols]
        right = jnp.concatenate(
            [product_rows(high_ref, low_ref, col_at[n], col_block, True) for n in near_cols + far_cols], axis=0
        )
        got = lax.dot_general(left, right, CONTRACT_LAST, preferred_element_type=jnp.float32)
        near[...] += got[:, :width]
        far[...] += got[:, width:]


def gram_rows(pieces, hot, hot_t, recip, row_at, col_at, place_at, row_block, col_block, orders):
    tiles, members, rows, lanes = pieces[0].shape
    groups, walkers = hot_t.shape
    hot = jnp.concatenate([hot, hot], axis=1)
    slots = len(orders[0])
    quarter = jax.ShapeDtypeStruct((slots * row_block, walkers // 4), jnp.float32)
    fixed = lambda t, *_: (0, 0)
    parts = pl.pallas_call(
        functools.partial(centre_kernel, row_block, col_block, orders, len(pieces)),
        out_shape=(quarter,) * 4,
        grid_spec=pltpu.PrefetchScalarGridSpec(
            num_scalar_prefetch=3,
            grid=(tiles // TOGETHER,),
            in_specs=[pl.BlockSpec((TOGETHER, members, rows, lanes), lambda t, *_: (t, 0, 0, 0))] * len(pieces)
            + [
                pl.BlockSpec((walkers, 2 * groups), fixed),
                pl.BlockSpec((groups, walkers), fixed),
                pl.BlockSpec((groups, 1), fixed),
            ],
            out_specs=(pl.BlockSpec(quarter.shape, fixed),) * 4,
            scratch_shapes=[
                pltpu.VMEM((TOGETHER, walkers, lanes), jnp.float32),
                pltpu.VMEM((TOGETHER, walkers, lanes), jnp.bfloat16),
                pltpu.VMEM((TOGETHER, walkers, lanes), jnp.bfloat16),
            ],
        ),
        compiler_params=pltpu.CompilerParams(vmem_limit_bytes=VMEM_LIMIT),
        name="gram_rows",
    )(row_at, col_at, place_at, *pieces, hot, hot_t, recip)
    return parts[:2], parts[2:]


def inverse_factor(value):
    size = value.shape[0]
    lane = lax.broadcasted_iota(jnp.int32, (1, size), 1)
    sub = lax.broadcasted_iota(jnp.int32, (SUB, 1), 0)
    tiles = [value[t * SUB : (t + 1) * SUB] for t in range(size // SUB)]
    for j in range(size):
        home, at = divmod(j, SUB)
        row = tiles[home][at : at + 1]
        scaled = jnp.where(lane == j, 1.0, row) / row[:, j : j + 1]
        for t in range(home, len(tiles)):
            tile = tiles[t]
            factor = tile[:, j : j + 1]
            clear = lane == j
            if t == home:
                if at == SUB - 1:
                    continue
                factor = jnp.where(sub > at, factor, 0.0)
                clear = clear & (sub > at)
            tiles[t] = jnp.where(clear, 0.0, tile) - factor * scaled
    value = jnp.concatenate(tiles, axis=0)
    row_id = lax.broadcasted_iota(jnp.int32, (size, 1), 0)
    diagonal = jnp.sum(jnp.where(lane == row_id, value, 0.0), axis=1, keepdims=True)
    unit = jnp.where(lane < row_id, value, jnp.where(lane == row_id, 1.0, 0.0))
    return unit / jnp.sqrt(diagonal)


def exact_dot(left, right, dims):
    return lax.dot_general(left, right, dims, precision=HIGHEST, preferred_element_type=jnp.float32)


def top_kernel(a_ref, inverse_ref, below_ref, rest_ref):
    half = inverse_ref.shape[0]
    inverse = inverse_factor(a_ref[:half, :half])
    inverse_ref[...] = inverse
    below = exact_dot(a_ref[half:, :half], inverse, CONTRACT_LAST)
    below_ref[...] = below
    rest_ref[...] = a_ref[half:, half:] - exact_dot(below, below, CONTRACT_LAST)


def low_kernel(top_ref, below_ref, rest_ref, out_ref):
    half = top_ref.shape[0]
    plain = (((1,), (0,)), ((), ()))
    inverse = inverse_factor(rest_ref[...])
    out_ref[:half, :half] = top_ref[...]
    out_ref[:half, half:] = jnp.zeros((half, half), jnp.float32)
    out_ref[half:, half:] = inverse
    out_ref[half:, :half] = -exact_dot(inverse, exact_dot(below_ref[...], top_ref[...], plain), plain)


def head_top(head):
    half = head.shape[0] // 2
    return pl.pallas_call(
        top_kernel, out_shape=[jax.ShapeDtypeStruct((half, half), jnp.float32)] * 3, name="head_top"
    )(head)


def head_low(top, below, rest):
    size = 2 * top.shape[0]
    return pl.pallas_call(
        low_kernel, out_shape=jax.ShapeDtypeStruct((size, size), jnp.float32), name="head_low"
    )(top, below, rest)


def on_device(features, signals, param_scale, geometry, electrons):
    par_size = lax.axis_size("par")
    walk_size = lax.axis_size("walk")
    walk_index = lax.axis_index("walk")
    par_index = lax.axis_index("par")
    per_device, slots_count, width = features.shape
    walkers = geometry.shape[0]
    groups = electrons.shape[0]
    row_block = per_device * par_size
    col_block = walkers // par_size
    plan = Plan(walk_size, par_size)

    anchor = (walk_index * par_size + par_index) * per_device
    own_geometry = lax.dynamic_slice_in_dim(geometry, anchor, per_device)
    own_matches = own_geometry[:, None] == jnp.arange(groups, dtype=jnp.int32)[None, :]
    own_electrons = jnp.sum(jnp.where(own_matches, electrons[None, :], 0), axis=1)
    live = (jnp.arange(slots_count, dtype=jnp.int32)[None, :] < own_electrons[:, None]).astype(jnp.float32)

    own = {"F": 0, "S": 0}
    for k, (axis, bit, kind) in enumerate(plan.dims):
        index = walk_index if axis == "walk" else par_index
        side = "F" if kind == "I" else "S"
        own[side] = own[side] + jnp.where((index & bit) != 0, 1 << plan.place[k], 0)
    flat = per_device * slots_count
    counts = (plan.blocks["F"], plan.blocks["S"])
    turned = turned_pieces(
        jnp.stack([own["F"], own["S"]]).astype(jnp.int32),
        live.reshape(1, flat),
        features.reshape(flat, width),
        signals.reshape(flat, width),
        counts,
    )
    names = [("F", 0, rb) for rb in range(counts[0])] + [("S", 0, rb) for rb in range(counts[1])]
    pieces = dict(zip(names, turned))
    ib, jb = width // plan.blocks["F"], width // plan.blocks["S"]
    parts = LANES // jb
    scaling = param_scale * (1.0 / math.sqrt(slots_count * width * width))
    scaling = lax.dynamic_slice(scaling, (own["F"] * ib, own["S"] * jb), (ib, jb))
    scaling = scaling.reshape(parts, ib // parts, jb).transpose(1, 0, 2).reshape(ib // parts, LANES)
    columns, names = exchange(plan, pieces, lambda f, s: jacobian(f, s, scaling, slots_count))
    place_at = []
    for src, core in [n for members in names for n in members]:
        walk_flip, par_flip = plan.flip(src)
        place_at.append((walk_index ^ (walk_flip | core)) * par_size + (par_index ^ par_flip))
    place_at = (jnp.stack(place_at) * per_device).astype(jnp.int32)

    matches = geometry[:, None] == jnp.arange(groups, dtype=jnp.int32)[None, :]
    hot = matches.astype(jnp.bfloat16)
    hot_t = (jnp.arange(groups, dtype=jnp.int32)[:, None] == geometry[None, :]).astype(jnp.bfloat16)
    counts = jnp.maximum(jnp.sum(matches.astype(jnp.float32), axis=0), 1.0)
    recip = (1.0 / counts)[:, None]

    chip_bits = walk_size.bit_length() - 2
    slots = 1 << chip_bits
    core, chip = walk_index & 1, walk_index >> 1
    row_at = jnp.stack([((chip ^ s) * 2 + core) * row_block for s in range(slots)]).astype(jnp.int32)
    col_at = jnp.stack([(par_index ^ p) * col_block for p in range(par_size)]).astype(jnp.int32)
    up = list(range(chip_bits))
    sweeps = (up, up[::-1])
    orders = tuple(
        tuple(sorted(range(slots), key=lambda s, o=o: [s >> b & 1 for b in o])) for o in sweeps
    )
    far, near = gram_rows(
        columns, hot, hot_t, recip, row_at, col_at, place_at, row_block, col_block, orders
    )

    def after(values, *others):
        tied = lax.optimization_barrier(tuple(values) + others)
        return list(tied[: len(values)])

    def plane_step(pair, step):
        mid = pair[0].shape[0] // 2
        return [permute(pair[h][mid:], "walk", walk_size, 2 << sweeps[h][step]) for h in range(2)]

    def plane_add(pair, moved):
        return [pair[h][: pair[h].shape[0] // 2] + moved[h] for h in range(2)]

    far, near = list(far), list(near)
    each = max(par_size // 4, 1)
    at = (par_index % each) * col_block
    head_cols = []
    for h in range(2):
        picked = None
        for q, part in enumerate(near + far):
            cols = lax.dynamic_slice(part, (0, at + h * PB // 2), (slots * row_block, PB // 2))
            if q % 2 != h:
                cols = cols.reshape(slots, row_block, PB // 2)
                cols = jnp.concatenate([cols[orders[q % 2].index(s)] for s in orders[h]], axis=0)
            picked = cols if picked is None else jnp.where(par_index // each == q, cols, picked)
        head_cols.append(picked)

    head_cols = plane_add(head_cols, plane_step(head_cols, 0))
    tied = after([*head_cols, *far, *near])
    head_cols, far, near = tied[:2], tied[2:4], tied[4:]
    far_moved = plane_step(far, 0)
    for step in range(1, chip_bits):
        head_cols = plane_add(head_cols, plane_step(head_cols, step))
    rows_mine = jnp.concatenate(head_cols, axis=1)
    bit = par_size // 2
    rows_mine = rows_mine + permute(rows_mine, "par", par_size, bit)
    far = plane_add(far, far_moved)
    rows_mine, far[0], far[1] = after([rows_mine, *far])
    for step in range(1, chip_bits):
        far_moved = plane_step(far, step)
        if step < chip_bits - 1:
            far = plane_add(far, far_moved)
    bit //= 2
    while bit:
        rows_mine = rows_mine + permute(rows_mine, "par", par_size, bit)
        bit //= 2

    chips = walk_size // 2
    per_col = col_block // row_block
    top_count = -(-PB // row_block)

    def spread(holder):
        total = jnp.where(chip == jnp.asarray([holder(z) for z in range(par_size)])[par_index], rows_mine, 0.0)
        for flip in range(1, chips):
            pairs = []
            for z in range(par_size):
                for c in range(2):
                    pairs.append(
                        ((holder(z) * 2 + c) * par_size + z, ((holder(z) ^ flip) * 2 + c) * par_size + z)
                    )
            total = total + lax.ppermute(rows_mine, ("walk", "par"), pairs)
        return total

    both = jnp.stack([spread(lambda z: 0), spread(lambda z: z)])
    far = plane_add(far, far_moved)
    both, far[0], far[1] = after([both, *far])
    far = [permute(part, "par", par_size, par_size // 2) for part in far]
    swapped = permute(both, "walk", walk_size, 1)
    swapped, near[0], near[1] = after([swapped, *near])
    near_moved = plane_step(near, 0)
    pair = [jnp.where(core == 0, both, swapped), jnp.where(core == 0, swapped, both)]
    head = jnp.concatenate([pair[0][0], pair[1][0]], axis=0)[:PB]
    col_rows = jnp.concatenate([pair[0][1], pair[1][1]], axis=0)

    def shift_at(first_row, count):
        ids = first_row + jnp.arange(count, dtype=jnp.int32)
        return SHIFT * (ids[:, None] == jnp.arange(PB, dtype=jnp.int32)[None, :]).astype(jnp.float32)

    first = head_top(head + shift_at(0, PB))
    near = plane_add(near, near_moved)
    tied = after([*first, *near])
    first, near = tied[:3], tied[3:]
    for step in range(1, chip_bits):
        near = plane_add(near, plane_step(near, step))
    inverse = head_low(*first)
    near = [part + got for part, got in zip(near, far)]
    moved = permute(near[1], "par", par_size, par_size // 4)
    inverse, near[0], near[1] = after([inverse, *near])
    own_panel = outer_rows(rows_mine + shift_at(walk_index * row_block, row_block), inverse)
    col_panel = outer_rows(col_rows + shift_at(par_index * col_block, col_block), inverse)
    update = outer_rows(own_panel, col_panel)
    gram = near[0] + moved
    bit = par_size // 8
    while bit:
        mid = gram.shape[1] // 2
        gram = gram[:, :mid] + permute(gram[:, mid:], "par", par_size, bit)
        bit //= 2
    row_ids = walk_index * row_block + jnp.arange(row_block, dtype=jnp.int32)
    col_ids = par_index * col_block + jnp.arange(col_block, dtype=jnp.int32)
    shifted = gram + SHIFT * (row_ids[:, None] == col_ids[None, :]).astype(jnp.float32)
    return (own_panel, shifted - update)


def solution(mesh):
    in_specs = (P(("walk", "par"), None, None), P(("walk", "par"), None, None), P(), P(), P())
    out_specs = (P("walk", None), P("walk", "par"))
    return jax.shard_map(
        on_device, mesh=mesh, in_specs=in_specs, out_specs=out_specs, check_vma=False
    )
```

```python
import functools
import math

import jax
import jax.numpy as jnp
import numpy as np
from jax import lax
from jax.experimental import pallas as pl
from jax.experimental.pallas import tpu as pltpu
from jax.sharding import PartitionSpec as P

PB = 256
HIGHEST = lax.Precision.HIGHEST
SHIFT = 0.05
LANES = 256
SUB = 8
TOGETHER = 2
CONTRACT_LAST = (((1,), (1,)), ((), ()))
VMEM_LIMIT = 60 * 1024 * 1024


def outer_rows(left_rows, right_rows):
    return lax.dot_general(left_rows, right_rows, CONTRACT_LAST, precision=HIGHEST)


def xor_pairs(size, bit):
    return [(i, i ^ bit) for i in range(size)]


class Plan:
    def __init__(self, walk_size, par_size):
        self.walk_size, self.par_size = walk_size, par_size
        par_bits = par_size.bit_length() - 1
        walk_bits = walk_size.bit_length() - 1
        self.dims = []
        for bit in reversed(range(par_bits)):
            self.dims.append(("par", 1 << bit, "J" if bit == 0 else "I"))
        for bit in range(1, walk_bits):
            self.dims.append(("walk", 1 << bit, "J" if bit == walk_bits - 1 else "I"))
        self.place = []
        seen = {"I": 0, "J": 0}
        for _, _, kind in self.dims:
            self.place.append(seen[kind])
            seen[kind] += 1
        self.blocks = {"F": 1 << seen["I"], "S": 1 << seen["J"]}
        self.order = {
            side: sorted(
                range(len(self.dims)), key=lambda k: (self.dims[k][0] == "walk", not self.splits(side, self.dims[k][2]))
            )
            for side in ("F", "S")
        }
        self.rounds = self.schedule()

    def splits(self, side, kind):
        return (side == "F") == (kind == "I")

    def depth(self, side, src, rb, after):
        best = 0
        order = self.order[side]
        for k in order[order.index(after) + 1 :]:
            if self.splits(side, self.dims[k][2]):
                if rb >> self.place[k] & 1:
                    return max(best, 1 + self.depth(side, src, rb ^ (1 << self.place[k]), k))
            else:
                best = max(best, 1 + self.depth(side, src, rb, k))
        return best

    def tasks(self):
        out = []
        for side in ("F", "S"):
            live = [(0, rb) for rb in range(self.blocks[side])]
            for k in self.order[side]:
                kind = self.dims[k][2]
                kept, made = [], []
                for src, rb in live:
                    if self.splits(side, kind):
                        p = self.place[k]
                        if rb >> p & 1:
                            made.append((k, (side, src, rb), (side, src | 1 << k, rb ^ (1 << p))))
                        else:
                            kept.append((src, rb))
                    else:
                        kept.append((src, rb))
                        made.append((k, (side, src, rb), (side, src | 1 << k, rb)))
                live = kept + [dst[1:] for _, _, dst in made]
                out += made
        return out

    def schedule(self):
        left = self.tasks()
        have = {(side, 0, rb) for side in ("F", "S") for rb in range(self.blocks[side])}
        rounds = []
        while left:
            chosen = []
            for k, (axis, _, _) in enumerate(self.dims):
                ready = [t for t in left if t[0] == k and t[1] in have]
                ready.sort(
                    key=lambda t: (
                        not self.splits(t[1][0], self.dims[k][2]),
                        axis == "par" and (t[2][1] & (self.par_size - 1)).bit_count(),
                        -self.depth(*t[2], k),
                    )
                )
                chosen += ready[: 1 if axis == "par" else 2]
            left = [t for t in left if t not in chosen]
            have |= {t[2] for t in chosen}
            rounds.append(chosen)
        return rounds

    def flip(self, src):
        walk = par = 0
        for k, (axis, bit, _) in enumerate(self.dims):
            if src >> k & 1:
                walk, par = (walk | bit, par) if axis == "walk" else (walk, par | bit)
        return walk, par


def permute(value, axis, size, bit):
    return lax.ppermute(value, axis, xor_pairs(size, bit))


def exchange(plan, pieces, block):
    sizes = {"walk": plan.walk_size, "par": plan.par_size}
    held = dict(pieces)
    planes, chips = plan.par_size, plan.walk_size // 2
    members = {q: [q | m * planes for m in range(chips)] for q in range(planes)}
    waiting = list(range(planes))
    own, other, sent = {}, {}, []
    gate = []
    rounds = list(plan.rounds)
    while rounds or waiting or sent:
        chosen = rounds.pop(0) if rounds else []
        groups = {}
        for k, src, dst in chosen:
            groups.setdefault((k, held[src].shape), []).append((src, dst))
        keys = sorted({s for pairs in groups.values() for s, _ in pairs})
        if keys and (gate or sent):
            tied = lax.optimization_barrier(
                tuple(held[n] for n in keys) + tuple(held[n] for n in gate) + tuple(own[q] for q in sent)
            )
            for n, v in zip(keys + gate, tied):
                held[n] = v
            for q, v in zip(sent, tied[len(keys) + len(gate) :]):
                own[q] = v
        gate = []
        for q in sent:
            other[q] = permute(own[q], "walk", plan.walk_size, 1)
        sent = []
        for q in list(waiting):
            if all((side, m, 0) in held for side in ("F", "S") for m in members[q]):
                own[q] = block([held["F", m, 0] for m in members[q]], [held["S", m, 0] for m in members[q]])
                waiting.remove(q)
                sent.append(q)
        for (k, _), pairs in groups.items():
            axis, bit, _ = plan.dims[k]
            if len(pairs) == 1:
                held[pairs[0][1]] = permute(held[pairs[0][0]], axis, sizes[axis], bit)
            else:
                moved = permute(jnp.stack([held[s] for s, _ in pairs]), axis, sizes[axis], bit)
                for i, (_, d) in enumerate(pairs):
                    held[d] = moved[i]
            gate += [d for _, d in pairs]
    return [own[q] for q in range(planes)] + [other[q] for q in range(planes)], [
        [(m, core) for m in members[q]] for core in range(2) for q in range(planes)
    ]


def turned_kernel(counts, own, live_ref, f_ref, s_ref, *refs):
    outs, turned_ref = refs[:-1], refs[-1]
    done = 0
    for side, (ref, count) in enumerate(zip((f_ref, s_ref), counts)):
        turned = ref[...].astype(jnp.float32).T
        turned_ref[...] = jnp.where(live_ref[...] > 0, turned, 0.0) if side == 0 else turned
        size = turned.shape[0] // count
        for rb in range(count):
            at = pl.multiple_of((own[side] ^ rb) * size, SUB)
            outs[done + rb][...] = turned_ref[pl.ds(at, size), :]
        done += count


def turned_pieces(own, live, features, signals, counts):
    rows, width = features.shape
    whole = pl.BlockSpec(memory_space=pltpu.VMEM)
    shapes = [jax.ShapeDtypeStruct((width // n, rows), jnp.float32) for n in counts for _ in range(n)]
    return pl.pallas_call(
        functools.partial(turned_kernel, counts),
        out_shape=shapes,
        in_specs=[pl.BlockSpec(memory_space=pltpu.SMEM), whole, whole, whole],
        out_specs=[whole] * len(shapes),
        scratch_shapes=[pltpu.VMEM((width, rows), jnp.float32)],
        compiler_params=pltpu.CompilerParams(vmem_limit_bytes=VMEM_LIMIT),
        name="turned_pieces",
    )(own, live, features, signals)


def jacobian_kernel(slots, count, *refs):
    lefts, rights, scale_ref, out_ref = refs[:count], refs[count : 2 * count], refs[2 * count], refs[-1]
    ib = lefts[0].shape[0]
    jb = rights[0].shape[0]
    together = LANES // slots
    parts = LANES // jb
    lane = lax.broadcasted_iota(jnp.int32, (together, LANES), 1)
    row = lax.broadcasted_iota(jnp.int32, (together, LANES), 0)
    mine = (lane >= row * slots) & (lane < row * slots + slots)
    for n in range(count):
        for g in range(lefts[n].shape[1] // LANES):
            left = lefts[n][:, g * LANES : (g + 1) * LANES]
            right = rights[n][:, g * LANES : (g + 1) * LANES].astype(jnp.bfloat16)
            spread = jnp.where(mine[None], left[:, None, :], 0.0).reshape(ib * together, LANES)
            block = lax.dot_general(
                spread.astype(jnp.bfloat16), right, CONTRACT_LAST, preferred_element_type=jnp.float32
            )
            block = block.reshape(parts, ib // parts, together, jb)
            for b in range(parts):
                out_ref[:, n, g * together : (g + 1) * together, b * jb : (b + 1) * jb] = (
                    block[b] * scale_ref[:, b * jb : (b + 1) * jb][:, None, :]
                )


def jacobian(lefts, rights, scaling, slots):
    count = len(lefts)
    ib, lanes = lefts[0].shape
    jb = rights[0].shape[0]
    tiles = ib * jb // LANES
    together = LANES // slots
    chunk = LANES * math.gcd(lanes // LANES, 3)
    return pl.pallas_call(
        functools.partial(jacobian_kernel, slots, count),
        out_shape=jax.ShapeDtypeStruct((tiles, count, lanes // slots, LANES), jnp.float32),
        grid=(lanes // chunk,),
        in_specs=[pl.BlockSpec((ib, chunk), lambda g: (0, g))] * count
        + [pl.BlockSpec((jb, chunk), lambda g: (0, g))] * count
        + [pl.BlockSpec((tiles, LANES), lambda g: (0, 0))],
        out_specs=pl.BlockSpec((tiles, count, chunk // slots, LANES), lambda g: (0, 0, g, 0)),
        compiler_params=pltpu.CompilerParams(vmem_limit_bytes=VMEM_LIMIT),
        name="jacobian",
    )(*lefts, *rights, scaling)


def split_two(value):
    high = value.astype(jnp.bfloat16)
    return high, (value - high.astype(jnp.float32)).astype(jnp.bfloat16)


def product_rows(high_ref, low_ref, at, size, swap):
    at = pl.ds(at if isinstance(at, int) else pl.multiple_of(at, 16), size)
    parts = []
    for i in range(high_ref.shape[0]):
        h, l = high_ref[i, at, :], low_ref[i, at, :]
        parts += [h, l, h] if swap else [h, h, l]
    return jnp.concatenate(parts, axis=1)


def centre_kernel(row_block, col_block, orders, count, row_at, col_at, place_at, *refs):
    pieces = refs[:count]
    hot_ref, hot_t_ref, recip_ref = refs[count : count + 3]
    far_a, far_b, near_a, near_b, value_ref, high_ref, low_ref = refs[count + 3 :]

    @pl.when(pl.program_id(0) == 0)
    def _():
        for ref in (far_a, far_b, near_a, near_b):
            ref[...] = jnp.zeros_like(ref)

    members, rows = pieces[0].shape[1:3]
    dot = functools.partial(jnp.dot, preferred_element_type=jnp.float32)
    for i in range(high_ref.shape[0]):
        for a in range(count):
            for m in range(members):
                at = pl.multiple_of(place_at[a * members + m], 8)
                value_ref[i, pl.ds(at, rows), :] = pieces[a][i, m]
        value = value_ref[i]
        high, low = split_two(value)
        means = (dot(hot_t_ref[...], high) + dot(hot_t_ref[...], low)) * recip_ref[...]
        means = jnp.concatenate(split_two(means), axis=0)
        high_ref[i], low_ref[i] = split_two(value - dot(hot_ref[...], means))

    blocks = col_at.shape[0]
    width = blocks // 4 * col_block
    for h, (far, near) in enumerate(((far_a, near_a), (far_b, near_b))):
        left = jnp.concatenate(
            [product_rows(high_ref, low_ref, row_at[s], row_block, False) for s in orders[h]], axis=0
        )
        near_cols = list(range(h * blocks // 4, (h + 1) * blocks // 4))
        far_cols = [n + blocks // 2 for n in near_cols]
        right = jnp.concatenate(
            [product_rows(high_ref, low_ref, col_at[n], col_block, True) for n in near_cols + far_cols], axis=0
        )
        got = lax.dot_general(left, right, CONTRACT_LAST, preferred_element_type=jnp.float32)
        near[...] += got[:, :width]
        far[...] += got[:, width:]


def gram_rows(pieces, hot, hot_t, recip, row_at, col_at, place_at, row_block, col_block, orders):
    tiles, members, rows, lanes = pieces[0].shape
    groups, walkers = hot_t.shape
    hot = jnp.concatenate([hot, hot], axis=1)
    slots = len(orders[0])
    quarter = jax.ShapeDtypeStruct((slots * row_block, walkers // 4), jnp.float32)
    fixed = lambda t, *_: (0, 0)
    parts = pl.pallas_call(
        functools.partial(centre_kernel, row_block, col_block, orders, len(pieces)),
        out_shape=(quarter,) * 4,
        grid_spec=pltpu.PrefetchScalarGridSpec(
            num_scalar_prefetch=3,
            grid=(tiles // TOGETHER,),
            in_specs=[pl.BlockSpec((TOGETHER, members, rows, lanes), lambda t, *_: (t, 0, 0, 0))] * len(pieces)
            + [
                pl.BlockSpec((walkers, 2 * groups), fixed),
                pl.BlockSpec((groups, walkers), fixed),
                pl.BlockSpec((groups, 1), fixed),
            ],
            out_specs=(pl.BlockSpec(quarter.shape, fixed),) * 4,
            scratch_shapes=[
                pltpu.VMEM((TOGETHER, walkers, lanes), jnp.float32),
                pltpu.VMEM((TOGETHER, walkers, lanes), jnp.bfloat16),
                pltpu.VMEM((TOGETHER, walkers, lanes), jnp.bfloat16),
            ],
        ),
        compiler_params=pltpu.CompilerParams(vmem_limit_bytes=VMEM_LIMIT),
        name="gram_rows",
    )(row_at, col_at, place_at, *pieces, hot, hot_t, recip)
    return parts[:2], parts[2:]


def inverse_factor(value):
    size = value.shape[0]
    lane = lax.broadcasted_iota(jnp.int32, (1, size), 1)
    sub = lax.broadcasted_iota(jnp.int32, (SUB, 1), 0)
    tiles = [value[t * SUB : (t + 1) * SUB] for t in range(size // SUB)]
    for j in range(size):
        home, at = divmod(j, SUB)
        row = tiles[home][at : at + 1]
        scaled = jnp.where(lane == j, 1.0, row) / row[:, j : j + 1]
        for t in range(home, len(tiles)):
            tile = tiles[t]
            factor = tile[:, j : j + 1]
            clear = lane == j
            if t == home:
                if at == SUB - 1:
                    continue
                factor = jnp.where(sub > at, factor, 0.0)
                clear = clear & (sub > at)
            tiles[t] = jnp.where(clear, 0.0, tile) - factor * scaled
    value = jnp.concatenate(tiles, axis=0)
    row_id = lax.broadcasted_iota(jnp.int32, (size, 1), 0)
    diagonal = jnp.sum(jnp.where(lane == row_id, value, 0.0), axis=1, keepdims=True)
    unit = jnp.where(lane < row_id, value, jnp.where(lane == row_id, 1.0, 0.0))
    return unit / jnp.sqrt(diagonal)


def exact_dot(left, right, dims):
    return lax.dot_general(left, right, dims, precision=HIGHEST, preferred_element_type=jnp.float32)


def top_kernel(a_ref, inverse_ref, below_ref, rest_ref):
    half = inverse_ref.shape[0]
    inverse = inverse_factor(a_ref[:half, :half])
    inverse_ref[...] = inverse
    below = exact_dot(a_ref[half:, :half], inverse, CONTRACT_LAST)
    below_ref[...] = below
    rest_ref[...] = a_ref[half:, half:] - exact_dot(below, below, CONTRACT_LAST)


def low_kernel(top_ref, below_ref, rest_ref, out_ref):
    half = top_ref.shape[0]
    plain = (((1,), (0,)), ((), ()))
    inverse = inverse_factor(rest_ref[...])
    out_ref[:half, :half] = top_ref[...]
    out_ref[:half, half:] = jnp.zeros((half, half), jnp.float32)
    out_ref[half:, half:] = inverse
    out_ref[half:, :half] = -exact_dot(inverse, exact_dot(below_ref[...], top_ref[...], plain), plain)


def head_top(head):
    half = head.shape[0] // 2
    return pl.pallas_call(
        top_kernel, out_shape=[jax.ShapeDtypeStruct((half, half), jnp.float32)] * 3, name="head_top"
    )(head)


def head_low(top, below, rest):
    size = 2 * top.shape[0]
    return pl.pallas_call(
        low_kernel, out_shape=jax.ShapeDtypeStruct((size, size), jnp.float32), name="head_low"
    )(top, below, rest)


def on_device(features, signals, param_scale, geometry, electrons):
    par_size = lax.axis_size("par")
    walk_size = lax.axis_size("walk")
    walk_index = lax.axis_index("walk")
    par_index = lax.axis_index("par")
    per_device, slots_count, width = features.shape
    walkers = geometry.shape[0]
    groups = electrons.shape[0]
    row_block = per_device * par_size
    col_block = walkers // par_size
    plan = Plan(walk_size, par_size)

    anchor = (walk_index * par_size + par_index) * per_device
    own_geometry = lax.dynamic_slice_in_dim(geometry, anchor, per_device)
    own_matches = own_geometry[:, None] == jnp.arange(groups, dtype=jnp.int32)[None, :]
    own_electrons = jnp.sum(jnp.where(own_matches, electrons[None, :], 0), axis=1)
    live = (jnp.arange(slots_count, dtype=jnp.int32)[None, :] < own_electrons[:, None]).astype(jnp.float32)

    own = {"F": 0, "S": 0}
    for k, (axis, bit, kind) in enumerate(plan.dims):
        index = walk_index if axis == "walk" else par_index
        side = "F" if kind == "I" else "S"
        own[side] = own[side] + jnp.where((index & bit) != 0, 1 << plan.place[k], 0)
    flat = per_device * slots_count
    counts = (plan.blocks["F"], plan.blocks["S"])
    turned = turned_pieces(
        jnp.stack([own["F"], own["S"]]).astype(jnp.int32),
        live.reshape(1, flat),
        features.reshape(flat, width),
        signals.reshape(flat, width),
        counts,
    )
    names = [("F", 0, rb) for rb in range(counts[0])] + [("S", 0, rb) for rb in range(counts[1])]
    pieces = dict(zip(names, turned))
    ib, jb = width // plan.blocks["F"], width // plan.blocks["S"]
    parts = LANES // jb
    scaling = param_scale * (1.0 / math.sqrt(slots_count * width * width))
    scaling = lax.dynamic_slice(scaling, (own["F"] * ib, own["S"] * jb), (ib, jb))
    scaling = scaling.reshape(parts, ib // parts, jb).transpose(1, 0, 2).reshape(ib // parts, LANES)
    columns, names = exchange(plan, pieces, lambda f, s: jacobian(f, s, scaling, slots_count))
    place_at = []
    for src, core in [n for members in names for n in members]:
        walk_flip, par_flip = plan.flip(src)
        place_at.append((walk_index ^ (walk_flip | core)) * par_size + (par_index ^ par_flip))
    place_at = (jnp.stack(place_at) * per_device).astype(jnp.int32)

    matches = geometry[:, None] == jnp.arange(groups, dtype=jnp.int32)[None, :]
    hot = matches.astype(jnp.bfloat16)
    hot_t = (jnp.arange(groups, dtype=jnp.int32)[:, None] == geometry[None, :]).astype(jnp.bfloat16)
    counts = jnp.maximum(jnp.sum(matches.astype(jnp.float32), axis=0), 1.0)
    recip = (1.0 / counts)[:, None]

    chip_bits = walk_size.bit_length() - 2
    slots = 1 << chip_bits
    core, chip = walk_index & 1, walk_index >> 1
    row_at = jnp.stack([((chip ^ s) * 2 + core) * row_block for s in range(slots)]).astype(jnp.int32)
    col_at = jnp.stack([(par_index ^ p) * col_block for p in range(par_size)]).astype(jnp.int32)
    up = list(range(chip_bits))
    sweeps = (up, up[::-1])
    orders = tuple(
        tuple(sorted(range(slots), key=lambda s, o=o: [s >> b & 1 for b in o])) for o in sweeps
    )
    far, near = gram_rows(
        columns, hot, hot_t, recip, row_at, col_at, place_at, row_block, col_block, orders
    )

    def after(values, *others):
        tied = lax.optimization_barrier(tuple(values) + others)
        return list(tied[: len(values)])

    def plane_step(pair, step):
        mid = pair[0].shape[0] // 2
        return [permute(pair[h][mid:], "walk", walk_size, 2 << sweeps[h][step]) for h in range(2)]

    def plane_add(pair, moved):
        return [pair[h][: pair[h].shape[0] // 2] + moved[h] for h in range(2)]

    far, near = list(far), list(near)
    each = max(par_size // 4, 1)
    at = (par_index % each) * col_block
    head_cols = []
    for h in range(2):
        picked = None
        for q, part in enumerate(near + far):
            cols = lax.dynamic_slice(part, (0, at + h * PB // 2), (slots * row_block, PB // 2))
            if q % 2 != h:
                cols = cols.reshape(slots, row_block, PB // 2)
                cols = jnp.concatenate([cols[orders[q % 2].index(s)] for s in orders[h]], axis=0)
            picked = cols if picked is None else jnp.where(par_index // each == q, cols, picked)
        head_cols.append(picked)

    head_cols = plane_add(head_cols, plane_step(head_cols, 0))
    tied = after([*head_cols, *far, *near])
    head_cols, far, near = tied[:2], tied[2:4], tied[4:]
    far_moved = plane_step(far, 0)
    for step in range(1, chip_bits):
        head_cols = plane_add(head_cols, plane_step(head_cols, step))
    rows_mine = jnp.concatenate(head_cols, axis=1)
    bit = par_size // 2
    rows_mine = rows_mine + permute(rows_mine, "par", par_size, bit)
    far = plane_add(far, far_moved)
    rows_mine, far[0], far[1] = after([rows_mine, *far])
    for step in range(1, chip_bits):
        far_moved = plane_step(far, step)
        if step < chip_bits - 1:
            far = plane_add(far, far_moved)
    bit //= 2
    while bit:
        rows_mine = rows_mine + permute(rows_mine, "par", par_size, bit)
        bit //= 2

    chips = walk_size // 2
    assert chips == par_size and col_block == 2 * row_block and row_block < PB <= 2 * row_block
    landed = [rows_mine]
    for flip in range(1, chips):
        pairs = []
        for z in range(par_size):
            for holder in sorted({0, z}):
                for c in range(2):
                    pairs.append(((holder * 2 + c) * par_size + z, ((holder ^ flip) * 2 + c) * par_size + z))
        landed.append(lax.ppermute(rows_mine, ("walk", "par"), pairs))
    landed = jnp.stack(landed)
    both = jnp.stack(
        [lax.dynamic_index_in_dim(landed, n, 0, keepdims=False) for n in (chip, chip ^ par_index)]
    )
    far = plane_add(far, far_moved)
    both, far[0], far[1] = after([both, *far])
    far = [permute(part, "par", par_size, par_size // 2) for part in far]
    swapped = permute(both, "walk", walk_size, 1)
    swapped, near[0], near[1] = after([swapped, *near])
    near_moved = plane_step(near, 0)
    pair = [jnp.where(core == 0, both, swapped), jnp.where(core == 0, swapped, both)]
    head = jnp.concatenate([pair[0][0], pair[1][0]], axis=0)[:PB]
    col_rows = jnp.concatenate([pair[0][1], pair[1][1]], axis=0)

    def shift_at(first_row, count):
        ids = first_row + jnp.arange(count, dtype=jnp.int32)
        return SHIFT * (ids[:, None] == jnp.arange(PB, dtype=jnp.int32)[None, :]).astype(jnp.float32)

    first = head_top(head + shift_at(0, PB))
    near = plane_add(near, near_moved)
    tied = after([*first, *near])
    first, near = tied[:3], tied[3:]
    for step in range(1, chip_bits):
        near = plane_add(near, plane_step(near, step))
    inverse = head_low(*first)
    near = [part + got for part, got in zip(near, far)]
    moved = permute(near[1], "par", par_size, par_size // 4)
    inverse, near[0], near[1] = after([inverse, *near])
    own_panel = outer_rows(rows_mine + shift_at(walk_index * row_block, row_block), inverse)
    col_panel = outer_rows(col_rows + shift_at(par_index * col_block, col_block), inverse)
    update = outer_rows(own_panel, col_panel)
    gram = near[0] + moved
    bit = par_size // 8
    while bit:
        mid = gram.shape[1] // 2
        gram = gram[:, :mid] + permute(gram[:, mid:], "par", par_size, bit)
        bit //= 2
    row_ids = walk_index * row_block + jnp.arange(row_block, dtype=jnp.int32)
    col_ids = par_index * col_block + jnp.arange(col_block, dtype=jnp.int32)
    shifted = gram + SHIFT * (row_ids[:, None] == col_ids[None, :]).astype(jnp.float32)
    return (own_panel, shifted - update)


def solution(mesh):
    in_specs = (P(("walk", "par"), None, None), P(("walk", "par"), None, None), P(), P(), P())
    out_specs = (P("walk", None), P("walk", "par"))
    return jax.shard_map(
        on_device, mesh=mesh, in_specs=in_specs, out_specs=out_specs, check_vma=False
    )
```

```python
import functools
import math

import jax
import jax.numpy as jnp
import numpy as np
from jax import lax
from jax.experimental import pallas as pl
from jax.experimental.pallas import tpu as pltpu
from jax.sharding import PartitionSpec as P

PB = 256
HIGHEST = lax.Precision.HIGHEST
SHIFT = 0.05
LANES = 256
SUB = 8
TOGETHER = 2
CONTRACT_LAST = (((1,), (1,)), ((), ()))
VMEM_LIMIT = 60 * 1024 * 1024


def outer_rows(left_rows, right_rows):
    return lax.dot_general(left_rows, right_rows, CONTRACT_LAST, precision=HIGHEST)


def xor_pairs(size, bit):
    return [(i, i ^ bit) for i in range(size)]


class Plan:
    def __init__(self, walk_size, par_size):
        self.walk_size, self.par_size = walk_size, par_size
        par_bits = par_size.bit_length() - 1
        walk_bits = walk_size.bit_length() - 1
        self.dims = []
        for bit in reversed(range(par_bits)):
            self.dims.append(("par", 1 << bit, "J" if bit == 0 else "I"))
        for bit in range(1, walk_bits):
            self.dims.append(("walk", 1 << bit, "J" if bit == walk_bits - 1 else "I"))
        self.place = []
        seen = {"I": 0, "J": 0}
        for _, _, kind in self.dims:
            self.place.append(seen[kind])
            seen[kind] += 1
        self.blocks = {"F": 1 << seen["I"], "S": 1 << seen["J"]}
        self.order = {
            side: sorted(
                range(len(self.dims)), key=lambda k: (self.dims[k][0] == "walk", not self.splits(side, self.dims[k][2]))
            )
            for side in ("F", "S")
        }
        self.rounds = self.schedule()

    def splits(self, side, kind):
        return (side == "F") == (kind == "I")

    def depth(self, side, src, rb, after):
        best = 0
        order = self.order[side]
        for k in order[order.index(after) + 1 :]:
            if self.splits(side, self.dims[k][2]):
                if rb >> self.place[k] & 1:
                    return max(best, 1 + self.depth(side, src, rb ^ (1 << self.place[k]), k))
            else:
                best = max(best, 1 + self.depth(side, src, rb, k))
        return best

    def tasks(self):
        out = []
        for side in ("F", "S"):
            live = [(0, rb) for rb in range(self.blocks[side])]
            for k in self.order[side]:
                kind = self.dims[k][2]
                kept, made = [], []
                for src, rb in live:
                    if self.splits(side, kind):
                        p = self.place[k]
                        if rb >> p & 1:
                            made.append((k, (side, src, rb), (side, src | 1 << k, rb ^ (1 << p))))
                        else:
                            kept.append((src, rb))
                    else:
                        kept.append((src, rb))
                        made.append((k, (side, src, rb), (side, src | 1 << k, rb)))
                live = kept + [dst[1:] for _, _, dst in made]
                out += made
        return out

    def schedule(self):
        left = self.tasks()
        have = {(side, 0, rb) for side in ("F", "S") for rb in range(self.blocks[side])}
        rounds = []
        while left:
            chosen = []
            for k, (axis, _, _) in enumerate(self.dims):
                ready = [t for t in left if t[0] == k and t[1] in have]
                ready.sort(
                    key=lambda t: (
                        not self.splits(t[1][0], self.dims[k][2]),
                        axis == "par" and (t[2][1] & (self.par_size - 1)).bit_count(),
                        -self.depth(*t[2], k),
                    )
                )
                chosen += ready[: 1 if axis == "par" else 2]
            left = [t for t in left if t not in chosen]
            have |= {t[2] for t in chosen}
            rounds.append(chosen)
        return rounds

    def flip(self, src):
        walk = par = 0
        for k, (axis, bit, _) in enumerate(self.dims):
            if src >> k & 1:
                walk, par = (walk | bit, par) if axis == "walk" else (walk, par | bit)
        return walk, par


def permute(value, axis, size, bit):
    return lax.ppermute(value, axis, xor_pairs(size, bit))


def exchange(plan, pieces, block):
    sizes = {"walk": plan.walk_size, "par": plan.par_size}
    held = dict(pieces)
    planes, chips = plan.par_size, plan.walk_size // 2
    members = {q: [q | m * planes for m in range(chips)] for q in range(planes)}
    waiting = list(range(planes))
    own, other, sent = {}, {}, []
    gate = []
    rounds = list(plan.rounds)
    while rounds or waiting or sent:
        chosen = rounds.pop(0) if rounds else []
        groups = {}
        for k, src, dst in chosen:
            groups.setdefault((k, held[src].shape), []).append((src, dst))
        keys = sorted({s for pairs in groups.values() for s, _ in pairs})
        if keys and (gate or sent):
            tied = lax.optimization_barrier(
                tuple(held[n] for n in keys) + tuple(held[n] for n in gate) + tuple(own[q] for q in sent)
            )
            for n, v in zip(keys + gate, tied):
                held[n] = v
            for q, v in zip(sent, tied[len(keys) + len(gate) :]):
                own[q] = v
        gate = []
        for q in sent:
            other[q] = permute(own[q], "walk", plan.walk_size, 1)
        sent = []
        for q in list(waiting):
            if all((side, m, 0) in held for side in ("F", "S") for m in members[q]):
                own[q] = block([held["F", m, 0] for m in members[q]], [held["S", m, 0] for m in members[q]])
                waiting.remove(q)
                sent.append(q)
        for (k, _), pairs in groups.items():
            axis, bit, _ = plan.dims[k]
            if len(pairs) == 1:
                held[pairs[0][1]] = permute(held[pairs[0][0]], axis, sizes[axis], bit)
            else:
                moved = permute(jnp.stack([held[s] for s, _ in pairs]), axis, sizes[axis], bit)
                for i, (_, d) in enumerate(pairs):
                    held[d] = moved[i]
            gate += [d for _, d in pairs]
    return [own[q] for q in range(planes)] + [other[q] for q in range(planes)], [
        [(m, core) for m in members[q]] for core in range(2) for q in range(planes)
    ]


def turned_kernel(counts, own, live_ref, f_ref, s_ref, *refs):
    outs, turned_ref = refs[:-1], refs[-1]
    done = 0
    for side, (ref, count) in enumerate(zip((f_ref, s_ref), counts)):
        turned = ref[...].astype(jnp.float32).T
        turned_ref[...] = jnp.where(live_ref[...] > 0, turned, 0.0) if side == 0 else turned
        size = turned.shape[0] // count
        for rb in range(count):
            at = pl.multiple_of((own[side] ^ rb) * size, SUB)
            outs[done + rb][...] = turned_ref[pl.ds(at, size), :]
        done += count


def turned_pieces(own, live, features, signals, counts):
    rows, width = features.shape
    whole = pl.BlockSpec(memory_space=pltpu.VMEM)
    shapes = [jax.ShapeDtypeStruct((width // n, rows), jnp.float32) for n in counts for _ in range(n)]
    return pl.pallas_call(
        functools.partial(turned_kernel, counts),
        out_shape=shapes,
        in_specs=[pl.BlockSpec(memory_space=pltpu.SMEM), whole, whole, whole],
        out_specs=[whole] * len(shapes),
        scratch_shapes=[pltpu.VMEM((width, rows), jnp.float32)],
        compiler_params=pltpu.CompilerParams(vmem_limit_bytes=VMEM_LIMIT),
        name="turned_pieces",
    )(own, live, features, signals)


def jacobian_kernel(slots, count, *refs):
    lefts, rights, scale_ref, out_ref = refs[:count], refs[count : 2 * count], refs[2 * count], refs[-1]
    ib = lefts[0].shape[0]
    jb = rights[0].shape[0]
    together = LANES // slots
    parts = LANES // jb
    lane = lax.broadcasted_iota(jnp.int32, (together, LANES), 1)
    row = lax.broadcasted_iota(jnp.int32, (together, LANES), 0)
    mine = (lane >= row * slots) & (lane < row * slots + slots)
    for n in range(count):
        for g in range(lefts[n].shape[1] // LANES):
            left = lefts[n][:, g * LANES : (g + 1) * LANES]
            right = rights[n][:, g * LANES : (g + 1) * LANES].astype(jnp.bfloat16)
            spread = jnp.where(mine[None], left[:, None, :], 0.0).reshape(ib * together, LANES)
            block = lax.dot_general(
                spread.astype(jnp.bfloat16), right, CONTRACT_LAST, preferred_element_type=jnp.float32
            )
            block = block.reshape(parts, ib // parts, together, jb)
            for b in range(parts):
                out_ref[:, n, g * together : (g + 1) * together, b * jb : (b + 1) * jb] = (
                    block[b] * scale_ref[:, b * jb : (b + 1) * jb][:, None, :]
                )


def jacobian(lefts, rights, scaling, slots):
    count = len(lefts)
    ib, lanes = lefts[0].shape
    jb = rights[0].shape[0]
    tiles = ib * jb // LANES
    together = LANES // slots
    chunk = LANES * math.gcd(lanes // LANES, 3)
    return pl.pallas_call(
        functools.partial(jacobian_kernel, slots, count),
        out_shape=jax.ShapeDtypeStruct((tiles, count, lanes // slots, LANES), jnp.float32),
        grid=(lanes // chunk,),
        in_specs=[pl.BlockSpec((ib, chunk), lambda g: (0, g))] * count
        + [pl.BlockSpec((jb, chunk), lambda g: (0, g))] * count
        + [pl.BlockSpec((tiles, LANES), lambda g: (0, 0))],
        out_specs=pl.BlockSpec((tiles, count, chunk // slots, LANES), lambda g: (0, 0, g, 0)),
        compiler_params=pltpu.CompilerParams(vmem_limit_bytes=VMEM_LIMIT),
        name="jacobian",
    )(*lefts, *rights, scaling)


def split_two(value):
    high = value.astype(jnp.bfloat16)
    return high, (value - high.astype(jnp.float32)).astype(jnp.bfloat16)


def product_rows(high_ref, low_ref, at, size, swap):
    at = pl.ds(at if isinstance(at, int) else pl.multiple_of(at, 16), size)
    parts = []
    for i in range(high_ref.shape[0]):
        h, l = high_ref[i, at, :], low_ref[i, at, :]
        parts += [h, l, h] if swap else [h, h, l]
    return jnp.concatenate(parts, axis=1)


def centre_kernel(row_block, col_block, orders, count, row_at, col_at, place_at, *refs):
    pieces = refs[:count]
    hot_ref, hot_t_ref, recip_ref = refs[count : count + 3]
    head_a, head_b, far_a, far_b, near_a, near_b, value_ref, high_ref, low_ref = refs[count + 3 :]

    @pl.when(pl.program_id(0) == 0)
    def _():
        for ref in (far_a, far_b, near_a, near_b):
            ref[...] = jnp.zeros_like(ref)

    members, rows = pieces[0].shape[1:3]
    dot = functools.partial(jnp.dot, preferred_element_type=jnp.float32)
    for i in range(high_ref.shape[0]):
        for a in range(count):
            for m in range(members):
                at = pl.multiple_of(place_at[a * members + m], 8)
                value_ref[i, pl.ds(at, rows), :] = pieces[a][i, m]
        value = value_ref[i]
        high, low = split_two(value)
        means = (dot(hot_t_ref[...], high) + dot(hot_t_ref[...], low)) * recip_ref[...]
        means = jnp.concatenate(split_two(means), axis=0)
        high_ref[i], low_ref[i] = split_two(value - dot(hot_ref[...], means))

    blocks = col_at.shape[0]
    width = blocks // 4 * col_block
    for h, (far, near) in enumerate(((far_a, near_a), (far_b, near_b))):
        left = jnp.concatenate(
            [product_rows(high_ref, low_ref, row_at[s], row_block, False) for s in orders[h]], axis=0
        )
        near_cols = list(range(h * blocks // 4, (h + 1) * blocks // 4))
        far_cols = [n + blocks // 2 for n in near_cols]
        right = jnp.concatenate(
            [product_rows(high_ref, low_ref, col_at[n], col_block, True) for n in near_cols + far_cols], axis=0
        )
        got = lax.dot_general(left, right, CONTRACT_LAST, preferred_element_type=jnp.float32)
        near[...] += got[:, :width]
        far[...] += got[:, width:]

    for n in range(blocks):
        part, own_order = ((near_a, 0), (near_b, 1), (far_a, 0), (far_b, 1))[n // (blocks // 4)]
        at = n % (blocks // 4) * col_block

        @pl.when((pl.program_id(0) == pl.num_programs(0) - 1) & (col_at[n] == 0))
        def _(part=part, own_order=own_order, at=at):
            for h, head in enumerate((head_a, head_b)):
                for i, s in enumerate(orders[h]):
                    j = orders[own_order].index(s)
                    head[i * row_block : (i + 1) * row_block, :] = part[
                        j * row_block : (j + 1) * row_block, at + h * PB // 2 : at + (h + 1) * PB // 2
                    ]


def gram_rows(pieces, hot, hot_t, recip, row_at, col_at, place_at, row_block, col_block, orders):
    tiles, members, rows, lanes = pieces[0].shape
    groups, walkers = hot_t.shape
    hot = jnp.concatenate([hot, hot], axis=1)
    slots = len(orders[0])
    quarter = jax.ShapeDtypeStruct((slots * row_block, walkers // 4), jnp.float32)
    head = jax.ShapeDtypeStruct((slots * row_block, PB // 2), jnp.float32)
    fixed = lambda t, *_: (0, 0)
    parts = pl.pallas_call(
        functools.partial(centre_kernel, row_block, col_block, orders, len(pieces)),
        out_shape=(head, head) + (quarter,) * 4,
        grid_spec=pltpu.PrefetchScalarGridSpec(
            num_scalar_prefetch=3,
            grid=(tiles // TOGETHER,),
            in_specs=[pl.BlockSpec((TOGETHER, members, rows, lanes), lambda t, *_: (t, 0, 0, 0))] * len(pieces)
            + [
                pl.BlockSpec((walkers, 2 * groups), fixed),
                pl.BlockSpec((groups, walkers), fixed),
                pl.BlockSpec((groups, 1), fixed),
            ],
            out_specs=(pl.BlockSpec(head.shape, fixed),) * 2 + (pl.BlockSpec(quarter.shape, fixed),) * 4,
            scratch_shapes=[
                pltpu.VMEM((TOGETHER, walkers, lanes), jnp.float32),
                pltpu.VMEM((TOGETHER, walkers, lanes), jnp.bfloat16),
                pltpu.VMEM((TOGETHER, walkers, lanes), jnp.bfloat16),
            ],
        ),
        compiler_params=pltpu.CompilerParams(vmem_limit_bytes=VMEM_LIMIT),
        name="gram_rows",
    )(row_at, col_at, place_at, *pieces, hot, hot_t, recip)
    return parts[:2], parts[2:4], parts[4:]


def inverse_factor(value):
    size = value.shape[0]
    lane = lax.broadcasted_iota(jnp.int32, (1, size), 1)
    sub = lax.broadcasted_iota(jnp.int32, (SUB, 1), 0)
    tiles = [value[t * SUB : (t + 1) * SUB] for t in range(size // SUB)]
    for j in range(size):
        home, at = divmod(j, SUB)
        row = tiles[home][at : at + 1]
        scaled = jnp.where(lane == j, 1.0, row) / row[:, j : j + 1]
        for t in range(home, len(tiles)):
            tile = tiles[t]
            factor = tile[:, j : j + 1]
            clear = lane == j
            if t == home:
                if at == SUB - 1:
                    continue
                factor = jnp.where(sub > at, factor, 0.0)
                clear = clear & (sub > at)
            tiles[t] = jnp.where(clear, 0.0, tile) - factor * scaled
    value = jnp.concatenate(tiles, axis=0)
    row_id = lax.broadcasted_iota(jnp.int32, (size, 1), 0)
    diagonal = jnp.sum(jnp.where(lane == row_id, value, 0.0), axis=1, keepdims=True)
    unit = jnp.where(lane < row_id, value, jnp.where(lane == row_id, 1.0, 0.0))
    return unit / jnp.sqrt(diagonal)


def exact_dot(left, right, dims):
    return lax.dot_general(left, right, dims, precision=HIGHEST, preferred_element_type=jnp.float32)


def top_kernel(a_ref, inverse_ref, below_ref, rest_ref):
    half = inverse_ref.shape[0]
    inverse = inverse_factor(a_ref[:half, :half])
    inverse_ref[...] = inverse
    below = exact_dot(a_ref[half:, :half], inverse, CONTRACT_LAST)
    below_ref[...] = below
    rest_ref[...] = a_ref[half:, half:] - exact_dot(below, below, CONTRACT_LAST)


def low_kernel(top_ref, below_ref, rest_ref, out_ref):
    half = top_ref.shape[0]
    plain = (((1,), (0,)), ((), ()))
    inverse = inverse_factor(rest_ref[...])
    out_ref[:half, :half] = top_ref[...]
    out_ref[:half, half:] = jnp.zeros((half, half), jnp.float32)
    out_ref[half:, half:] = inverse
    out_ref[half:, :half] = -exact_dot(inverse, exact_dot(below_ref[...], top_ref[...], plain), plain)


def head_top(head):
    half = head.shape[0] // 2
    return pl.pallas_call(
        top_kernel, out_shape=[jax.ShapeDtypeStruct((half, half), jnp.float32)] * 3, name="head_top"
    )(head)


def head_low(top, below, rest):
    size = 2 * top.shape[0]
    return pl.pallas_call(
        low_kernel, out_shape=jax.ShapeDtypeStruct((size, size), jnp.float32), name="head_low"
    )(top, below, rest)


def on_device(features, signals, param_scale, geometry, electrons):
    par_size = lax.axis_size("par")
    walk_size = lax.axis_size("walk")
    walk_index = lax.axis_index("walk")
    par_index = lax.axis_index("par")
    per_device, slots_count, width = features.shape
    walkers = geometry.shape[0]
    groups = electrons.shape[0]
    row_block = per_device * par_size
    col_block = walkers // par_size
    plan = Plan(walk_size, par_size)

    anchor = (walk_index * par_size + par_index) * per_device
    own_geometry = lax.dynamic_slice_in_dim(geometry, anchor, per_device)
    own_matches = own_geometry[:, None] == jnp.arange(groups, dtype=jnp.int32)[None, :]
    own_electrons = jnp.sum(jnp.where(own_matches, electrons[None, :], 0), axis=1)
    live = (jnp.arange(slots_count, dtype=jnp.int32)[None, :] < own_electrons[:, None]).astype(jnp.float32)

    own = {"F": 0, "S": 0}
    for k, (axis, bit, kind) in enumerate(plan.dims):
        index = walk_index if axis == "walk" else par_index
        side = "F" if kind == "I" else "S"
        own[side] = own[side] + jnp.where((index & bit) != 0, 1 << plan.place[k], 0)
    flat = per_device * slots_count
    counts = (plan.blocks["F"], plan.blocks["S"])
    turned = turned_pieces(
        jnp.stack([own["F"], own["S"]]).astype(jnp.int32),
        live.reshape(1, flat),
        features.reshape(flat, width),
        signals.reshape(flat, width),
        counts,
    )
    names = [("F", 0, rb) for rb in range(counts[0])] + [("S", 0, rb) for rb in range(counts[1])]
    pieces = dict(zip(names, turned))
    ib, jb = width // plan.blocks["F"], width // plan.blocks["S"]
    parts = LANES // jb
    scaling = param_scale * (1.0 / math.sqrt(slots_count * width * width))
    scaling = lax.dynamic_slice(scaling, (own["F"] * ib, own["S"] * jb), (ib, jb))
    scaling = scaling.reshape(parts, ib // parts, jb).transpose(1, 0, 2).reshape(ib // parts, LANES)
    columns, names = exchange(plan, pieces, lambda f, s: jacobian(f, s, scaling, slots_count))
    place_at = []
    for src, core in [n for members in names for n in members]:
        walk_flip, par_flip = plan.flip(src)
        place_at.append((walk_index ^ (walk_flip | core)) * par_size + (par_index ^ par_flip))
    place_at = (jnp.stack(place_at) * per_device).astype(jnp.int32)

    matches = geometry[:, None] == jnp.arange(groups, dtype=jnp.int32)[None, :]
    hot = matches.astype(jnp.bfloat16)
    hot_t = (jnp.arange(groups, dtype=jnp.int32)[:, None] == geometry[None, :]).astype(jnp.bfloat16)
    counts = jnp.maximum(jnp.sum(matches.astype(jnp.float32), axis=0), 1.0)
    recip = (1.0 / counts)[:, None]

    chip_bits = walk_size.bit_length() - 2
    slots = 1 << chip_bits
    core, chip = walk_index & 1, walk_index >> 1
    row_at = jnp.stack([((chip ^ s) * 2 + core) * row_block for s in range(slots)]).astype(jnp.int32)
    col_at = jnp.stack([(par_index ^ p) * col_block for p in range(par_size)]).astype(jnp.int32)
    up = list(range(chip_bits))
    sweeps = (up, up[::-1])
    orders = tuple(
        tuple(sorted(range(slots), key=lambda s, o=o: [s >> b & 1 for b in o])) for o in sweeps
    )
    head_cols, far, near = gram_rows(
        columns, hot, hot_t, recip, row_at, col_at, place_at, row_block, col_block, orders
    )

    def after(values, *others):
        tied = lax.optimization_barrier(tuple(values) + others)
        return list(tied[: len(values)])

    def plane_step(pair, step):
        mid = pair[0].shape[0] // 2
        return [permute(pair[h][mid:], "walk", walk_size, 2 << sweeps[h][step]) for h in range(2)]

    def plane_add(pair, moved):
        return [pair[h][: pair[h].shape[0] // 2] + moved[h] for h in range(2)]

    far, near = list(far), list(near)
    head_cols = plane_add(head_cols, plane_step(head_cols, 0))
    tied = after([*head_cols, *far, *near])
    head_cols, far, near = tied[:2], tied[2:4], tied[4:]
    far_moved = plane_step(far, 0)
    for step in range(1, chip_bits):
        head_cols = plane_add(head_cols, plane_step(head_cols, step))
    rows_mine = jnp.concatenate(head_cols, axis=1)
    bit = par_size // 2
    rows_mine = rows_mine + permute(rows_mine, "par", par_size, bit)
    far = plane_add(far, far_moved)
    rows_mine, far[0], far[1] = after([rows_mine, *far])
    for step in range(1, chip_bits):
        far_moved = plane_step(far, step)
        if step < chip_bits - 1:
            far = plane_add(far, far_moved)
    bit //= 2
    while bit:
        rows_mine = rows_mine + permute(rows_mine, "par", par_size, bit)
        bit //= 2

    chips = walk_size // 2
    assert chips == par_size and col_block == 2 * row_block and row_block < PB <= 2 * row_block
    landed = [rows_mine]
    for flip in range(1, chips):
        pairs = []
        for z in range(par_size):
            for holder in sorted({0, z}):
                for c in range(2):
                    pairs.append(((holder * 2 + c) * par_size + z, ((holder ^ flip) * 2 + c) * par_size + z))
        landed.append(lax.ppermute(rows_mine, ("walk", "par"), pairs))
    landed = jnp.stack(landed)
    both = jnp.stack(
        [lax.dynamic_index_in_dim(landed, n, 0, keepdims=False) for n in (chip, chip ^ par_index)]
    )
    far = plane_add(far, far_moved)
    both, far[0], far[1] = after([both, *far])
    far = [permute(part, "par", par_size, par_size // 2) for part in far]
    swapped = permute(both, "walk", walk_size, 1)
    swapped, near[0], near[1] = after([swapped, *near])
    near_moved = plane_step(near, 0)
    pair = [jnp.where(core == 0, both, swapped), jnp.where(core == 0, swapped, both)]
    head = jnp.concatenate([pair[0][0], pair[1][0]], axis=0)[:PB]
    col_rows = jnp.concatenate([pair[0][1], pair[1][1]], axis=0)

    def shift_at(first_row, count):
        ids = first_row + jnp.arange(count, dtype=jnp.int32)
        return SHIFT * (ids[:, None] == jnp.arange(PB, dtype=jnp.int32)[None, :]).astype(jnp.float32)

    first = head_top(head + shift_at(0, PB))
    near = plane_add(near, near_moved)
    tied = after([*first, *near])
    first, near = tied[:3], tied[3:]
    for step in range(1, chip_bits):
        near = plane_add(near, plane_step(near, step))
    inverse = head_low(*first)
    near = [part + got for part, got in zip(near, far)]
    moved = permute(near[1], "par", par_size, par_size // 4)
    inverse, near[0], near[1] = after([inverse, *near])
    panels = outer_rows(
        jnp.concatenate(
            [
                rows_mine + shift_at(walk_index * row_block, row_block),
                col_rows + shift_at(par_index * col_block, col_block),
            ],
            axis=0,
        ),
        inverse,
    )
    own_panel, col_panel = panels[:row_block], panels[row_block:]
    update = outer_rows(own_panel, col_panel)
    gram = near[0] + moved
    bit = par_size // 8
    while bit:
        mid = gram.shape[1] // 2
        gram = gram[:, :mid] + permute(gram[:, mid:], "par", par_size, bit)
        bit //= 2
    row_ids = walk_index * row_block + jnp.arange(row_block, dtype=jnp.int32)
    col_ids = par_index * col_block + jnp.arange(col_block, dtype=jnp.int32)
    shifted = gram + SHIFT * (row_ids[:, None] == col_ids[None, :]).astype(jnp.float32)
    return (own_panel, shifted - update)


def solution(mesh):
    in_specs = (P(("walk", "par"), None, None), P(("walk", "par"), None, None), P(), P(), P())
    out_specs = (P("walk", None), P("walk", "par"))
    return jax.shard_map(
        on_device, mesh=mesh, in_specs=in_specs, out_specs=out_specs, check_vma=False
    )
```

```python
import functools
import math

import jax
import jax.numpy as jnp
import numpy as np
from jax import lax
from jax.experimental import pallas as pl
from jax.experimental.pallas import tpu as pltpu
from jax.sharding import PartitionSpec as P

PB = 256
HIGHEST = lax.Precision.HIGHEST
SHIFT = 0.05
LANES = 256
SUB = 8
TOGETHER = 2
CONTRACT_LAST = (((1,), (1,)), ((), ()))
VMEM_LIMIT = 60 * 1024 * 1024


def outer_rows(left_rows, right_rows):
    return lax.dot_general(left_rows, right_rows, CONTRACT_LAST, precision=HIGHEST)


def xor_pairs(size, bit):
    return [(i, i ^ bit) for i in range(size)]


class Plan:
    def __init__(self, walk_size, par_size):
        self.walk_size, self.par_size = walk_size, par_size
        par_bits = par_size.bit_length() - 1
        walk_bits = walk_size.bit_length() - 1
        self.dims = []
        for bit in reversed(range(par_bits)):
            self.dims.append(("par", 1 << bit, "J" if bit == 0 else "I"))
        for bit in range(1, walk_bits):
            self.dims.append(("walk", 1 << bit, "J" if bit == walk_bits - 1 else "I"))
        self.place = []
        seen = {"I": 0, "J": 0}
        for _, _, kind in self.dims:
            self.place.append(seen[kind])
            seen[kind] += 1
        self.blocks = {"F": 1 << seen["I"], "S": 1 << seen["J"]}
        self.order = {
            side: sorted(
                range(len(self.dims)), key=lambda k: (self.dims[k][0] == "walk", not self.splits(side, self.dims[k][2]))
            )
            for side in ("F", "S")
        }
        self.rounds = self.schedule()

    def splits(self, side, kind):
        return (side == "F") == (kind == "I")

    def depth(self, side, src, rb, after):
        best = 0
        order = self.order[side]
        for k in order[order.index(after) + 1 :]:
            if self.splits(side, self.dims[k][2]):
                if rb >> self.place[k] & 1:
                    return max(best, 1 + self.depth(side, src, rb ^ (1 << self.place[k]), k))
            else:
                best = max(best, 1 + self.depth(side, src, rb, k))
        return best

    def tasks(self):
        out = []
        for side in ("F", "S"):
            live = [(0, rb) for rb in range(self.blocks[side])]
            for k in self.order[side]:
                kind = self.dims[k][2]
                kept, made = [], []
                for src, rb in live:
                    if self.splits(side, kind):
                        p = self.place[k]
                        if rb >> p & 1:
                            made.append((k, (side, src, rb), (side, src | 1 << k, rb ^ (1 << p))))
                        else:
                            kept.append((src, rb))
                    else:
                        kept.append((src, rb))
                        made.append((k, (side, src, rb), (side, src | 1 << k, rb)))
                live = kept + [dst[1:] for _, _, dst in made]
                out += made
        return out

    def schedule(self):
        left = self.tasks()
        have = {(side, 0, rb) for side in ("F", "S") for rb in range(self.blocks[side])}
        rounds = []
        while left:
            chosen = []
            for k, (axis, _, _) in enumerate(self.dims):
                ready = [t for t in left if t[0] == k and t[1] in have]
                ready.sort(
                    key=lambda t: (
                        not self.splits(t[1][0], self.dims[k][2]),
                        axis == "par" and (t[2][1] & (self.par_size - 1)).bit_count(),
                        -self.depth(*t[2], k),
                    )
                )
                chosen += ready[: 1 if axis == "par" else 2]
            left = [t for t in left if t not in chosen]
            have |= {t[2] for t in chosen}
            rounds.append(chosen)
        return rounds

    def flip(self, src):
        walk = par = 0
        for k, (axis, bit, _) in enumerate(self.dims):
            if src >> k & 1:
                walk, par = (walk | bit, par) if axis == "walk" else (walk, par | bit)
        return walk, par


def permute(value, axis, size, bit):
    return lax.ppermute(value, axis, xor_pairs(size, bit))


def exchange(plan, pieces, block):
    sizes = {"walk": plan.walk_size, "par": plan.par_size}
    held = dict(pieces)
    planes, chips = plan.par_size, plan.walk_size // 2
    members = {q: [q | m * planes for m in range(chips)] for q in range(planes)}
    waiting = list(range(planes))
    own, other, sent = {}, {}, []
    gate = []
    rounds = list(plan.rounds)
    while rounds or waiting or sent:
        chosen = rounds.pop(0) if rounds else []
        groups = {}
        for k, src, dst in chosen:
            groups.setdefault((k, held[src].shape), []).append((src, dst))
        keys = sorted({s for pairs in groups.values() for s, _ in pairs})
        if keys and (gate or sent):
            tied = lax.optimization_barrier(
                tuple(held[n] for n in keys) + tuple(held[n] for n in gate) + tuple(own[q] for q in sent)
            )
            for n, v in zip(keys + gate, tied):
                held[n] = v
            for q, v in zip(sent, tied[len(keys) + len(gate) :]):
                own[q] = v
        gate = []
        for q in sent:
            other[q] = permute(own[q], "walk", plan.walk_size, 1)
        sent = []
        for q in list(waiting):
            if all((side, m, 0) in held for side in ("F", "S") for m in members[q]):
                own[q] = block([held["F", m, 0] for m in members[q]], [held["S", m, 0] for m in members[q]])
                waiting.remove(q)
                sent.append(q)
        for (k, _), pairs in groups.items():
            axis, bit, _ = plan.dims[k]
            if len(pairs) == 1:
                held[pairs[0][1]] = permute(held[pairs[0][0]], axis, sizes[axis], bit)
            else:
                moved = permute(jnp.stack([held[s] for s, _ in pairs]), axis, sizes[axis], bit)
                for i, (_, d) in enumerate(pairs):
                    held[d] = moved[i]
            gate += [d for _, d in pairs]
    return [own[q] for q in range(planes)] + [other[q] for q in range(planes)], [
        [(m, core) for m in members[q]] for core in range(2) for q in range(planes)
    ]


def turned_kernel(counts, own, live_ref, f_ref, s_ref, *refs):
    outs, turned_ref = refs[:-1], refs[-1]
    done = 0
    for side, (ref, count) in enumerate(zip((f_ref, s_ref), counts)):
        turned = ref[...].astype(jnp.float32).T
        turned_ref[...] = jnp.where(live_ref[...] > 0, turned, 0.0) if side == 0 else turned
        size = turned.shape[0] // count
        for rb in range(count):
            at = pl.multiple_of((own[side] ^ rb) * size, SUB)
            outs[done + rb][...] = turned_ref[pl.ds(at, size), :]
        done += count


def turned_pieces(own, live, features, signals, counts):
    rows, width = features.shape
    whole = pl.BlockSpec(memory_space=pltpu.VMEM)
    shapes = [jax.ShapeDtypeStruct((width // n, rows), jnp.float32) for n in counts for _ in range(n)]
    return pl.pallas_call(
        functools.partial(turned_kernel, counts),
        out_shape=shapes,
        in_specs=[pl.BlockSpec(memory_space=pltpu.SMEM), whole, whole, whole],
        out_specs=[whole] * len(shapes),
        scratch_shapes=[pltpu.VMEM((width, rows), jnp.float32)],
        compiler_params=pltpu.CompilerParams(vmem_limit_bytes=VMEM_LIMIT),
        name="turned_pieces",
    )(own, live, features, signals)


def jacobian_kernel(slots, count, *refs):
    lefts, rights, scale_ref, out_ref = refs[:count], refs[count : 2 * count], refs[2 * count], refs[-1]
    ib = lefts[0].shape[0]
    jb = rights[0].shape[0]
    together = LANES // slots
    parts = LANES // jb
    lane = lax.broadcasted_iota(jnp.int32, (together, LANES), 1)
    row = lax.broadcasted_iota(jnp.int32, (together, LANES), 0)
    mine = (lane >= row * slots) & (lane < row * slots + slots)
    for n in range(count):
        for g in range(lefts[n].shape[1] // LANES):
            left = lefts[n][:, g * LANES : (g + 1) * LANES]
            right = rights[n][:, g * LANES : (g + 1) * LANES].astype(jnp.bfloat16)
            spread = jnp.where(mine[None], left[:, None, :], 0.0).reshape(ib * together, LANES)
            block = lax.dot_general(
                spread.astype(jnp.bfloat16), right, CONTRACT_LAST, preferred_element_type=jnp.float32
            )
            block = block.reshape(parts, ib // parts, together, jb)
            for b in range(parts):
                out_ref[:, n, g * together : (g + 1) * together, b * jb : (b + 1) * jb] = (
                    block[b] * scale_ref[:, b * jb : (b + 1) * jb][:, None, :]
                )


def jacobian(lefts, rights, scaling, slots):
    count = len(lefts)
    ib, lanes = lefts[0].shape
    jb = rights[0].shape[0]
    tiles = ib * jb // LANES
    together = LANES // slots
    chunk = LANES * math.gcd(lanes // LANES, 3)
    return pl.pallas_call(
        functools.partial(jacobian_kernel, slots, count),
        out_shape=jax.ShapeDtypeStruct((tiles, count, lanes // slots, LANES), jnp.float32),
        grid=(lanes // chunk,),
        in_specs=[pl.BlockSpec((ib, chunk), lambda g: (0, g))] * count
        + [pl.BlockSpec((jb, chunk), lambda g: (0, g))] * count
        + [pl.BlockSpec((tiles, LANES), lambda g: (0, 0))],
        out_specs=pl.BlockSpec((tiles, count, chunk // slots, LANES), lambda g: (0, 0, g, 0)),
        compiler_params=pltpu.CompilerParams(vmem_limit_bytes=VMEM_LIMIT),
        name="jacobian",
    )(*lefts, *rights, scaling)


def split_two(value):
    high = value.astype(jnp.bfloat16)
    return high, (value - high.astype(jnp.float32)).astype(jnp.bfloat16)


def product_rows(high_ref, low_ref, at, size, swap):
    at = pl.ds(at if isinstance(at, int) else pl.multiple_of(at, 16), size)
    parts = []
    for i in range(high_ref.shape[0]):
        h, l = high_ref[i, at, :], low_ref[i, at, :]
        parts += [h, l, h] if swap else [h, h, l]
    return jnp.concatenate(parts, axis=1)


def centre_kernel(row_block, col_block, orders, count, row_at, col_at, place_at, *refs):
    pieces = refs[:count]
    hot_ref, hot_t_ref, recip_ref = refs[count : count + 3]
    head_a, head_b, far_a, far_b, near_a, near_b, value_ref, high_ref, low_ref = refs[count + 3 :]

    @pl.when(pl.program_id(0) == 0)
    def _():
        for ref in (far_a, far_b, near_a, near_b):
            ref[...] = jnp.zeros_like(ref)

    members, rows = pieces[0].shape[1:3]
    dot = functools.partial(jnp.dot, preferred_element_type=jnp.float32)
    for i in range(high_ref.shape[0]):
        for a in range(count):
            for m in range(members):
                at = pl.multiple_of(place_at[a * members + m], 8)
                value_ref[i, pl.ds(at, rows), :] = pieces[a][i, m]
        value = value_ref[i]
        high, low = split_two(value)
        means = (dot(hot_t_ref[...], high) + dot(hot_t_ref[...], low)) * recip_ref[...]
        means = jnp.concatenate(split_two(means), axis=0)
        high_ref[i], low_ref[i] = split_two(value - dot(hot_ref[...], means))

    blocks = col_at.shape[0]
    width = blocks // 4 * col_block
    for h, (far, near) in enumerate(((far_a, near_a), (far_b, near_b))):
        left = jnp.concatenate(
            [product_rows(high_ref, low_ref, row_at[s], row_block, False) for s in orders[h]], axis=0
        )
        near_cols = list(range(h * blocks // 4, (h + 1) * blocks // 4))
        far_cols = [n + blocks // 2 for n in near_cols]
        right = jnp.concatenate(
            [product_rows(high_ref, low_ref, col_at[n], col_block, True) for n in near_cols + far_cols], axis=0
        )
        got = lax.dot_general(left, right, CONTRACT_LAST, preferred_element_type=jnp.float32)
        near[...] += got[:, :width]
        far[...] += got[:, width:]

    for n in range(blocks):
        part, own_order = ((near_a, 0), (near_b, 1), (far_a, 0), (far_b, 1))[n // (blocks // 4)]
        at = n % (blocks // 4) * col_block

        @pl.when((pl.program_id(0) == pl.num_programs(0) - 1) & (col_at[n] == 0))
        def _(part=part, own_order=own_order, at=at):
            for h, head in enumerate((head_a, head_b)):
                for i, s in enumerate(orders[h]):
                    j = orders[own_order].index(s)
                    head[i * row_block : (i + 1) * row_block, :] = part[
                        j * row_block : (j + 1) * row_block, at + h * PB // 2 : at + (h + 1) * PB // 2
                    ]


def gram_rows(pieces, hot, hot_t, recip, row_at, col_at, place_at, row_block, col_block, orders):
    tiles, members, rows, lanes = pieces[0].shape
    groups, walkers = hot_t.shape
    hot = jnp.concatenate([hot, hot], axis=1)
    slots = len(orders[0])
    quarter = jax.ShapeDtypeStruct((slots * row_block, walkers // 4), jnp.float32)
    head = jax.ShapeDtypeStruct((slots * row_block, PB // 2), jnp.float32)
    fixed = lambda t, *_: (0, 0)
    parts = pl.pallas_call(
        functools.partial(centre_kernel, row_block, col_block, orders, len(pieces)),
        out_shape=(head, head) + (quarter,) * 4,
        grid_spec=pltpu.PrefetchScalarGridSpec(
            num_scalar_prefetch=3,
            grid=(tiles // TOGETHER,),
            in_specs=[pl.BlockSpec((TOGETHER, members, rows, lanes), lambda t, *_: (t, 0, 0, 0))] * len(pieces)
            + [
                pl.BlockSpec((walkers, 2 * groups), fixed),
                pl.BlockSpec((groups, walkers), fixed),
                pl.BlockSpec((groups, 1), fixed),
            ],
            out_specs=(pl.BlockSpec(head.shape, fixed),) * 2 + (pl.BlockSpec(quarter.shape, fixed),) * 4,
            scratch_shapes=[
                pltpu.VMEM((TOGETHER, walkers, lanes), jnp.float32),
                pltpu.VMEM((TOGETHER, walkers, lanes), jnp.bfloat16),
                pltpu.VMEM((TOGETHER, walkers, lanes), jnp.bfloat16),
            ],
        ),
        compiler_params=pltpu.CompilerParams(vmem_limit_bytes=VMEM_LIMIT),
        name="gram_rows",
    )(row_at, col_at, place_at, *pieces, hot, hot_t, recip)
    return parts[:2], parts[2:4], parts[4:]


def inverse_factor(value):
    size = value.shape[0]
    lane = lax.broadcasted_iota(jnp.int32, (1, size), 1)
    sub = lax.broadcasted_iota(jnp.int32, (SUB, 1), 0)
    tiles = [value[t * SUB : (t + 1) * SUB] for t in range(size // SUB)]
    for j in range(size):
        home, at = divmod(j, SUB)
        row = tiles[home][at : at + 1]
        scaled = jnp.where(lane == j, 1.0, row) / row[:, j : j + 1]
        for t in range(home, len(tiles)):
            tile = tiles[t]
            factor = tile[:, j : j + 1]
            clear = lane == j
            if t == home:
                if at == SUB - 1:
                    continue
                factor = jnp.where(sub > at, factor, 0.0)
                clear = clear & (sub > at)
            tiles[t] = jnp.where(clear, 0.0, tile) - factor * scaled
    value = jnp.concatenate(tiles, axis=0)
    row_id = lax.broadcasted_iota(jnp.int32, (size, 1), 0)
    diagonal = jnp.sum(jnp.where(lane == row_id, value, 0.0), axis=1, keepdims=True)
    unit = jnp.where(lane < row_id, value, jnp.where(lane == row_id, 1.0, 0.0))
    return unit / jnp.sqrt(diagonal)


def exact_dot(left, right, dims):
    return lax.dot_general(left, right, dims, precision=HIGHEST, preferred_element_type=jnp.float32)


def top_kernel(a_ref, inverse_ref, below_ref, rest_ref):
    half = inverse_ref.shape[0]
    inverse = inverse_factor(a_ref[:half, :half])
    inverse_ref[...] = inverse
    below = exact_dot(a_ref[half:, :half], inverse, CONTRACT_LAST)
    below_ref[...] = below
    rest_ref[...] = a_ref[half:, half:] - exact_dot(below, below, CONTRACT_LAST)


def low_kernel(top_ref, below_ref, rest_ref, out_ref):
    half = top_ref.shape[0]
    plain = (((1,), (0,)), ((), ()))
    inverse = inverse_factor(rest_ref[...])
    out_ref[:half, :half] = top_ref[...]
    out_ref[:half, half:] = jnp.zeros((half, half), jnp.float32)
    out_ref[half:, half:] = inverse
    out_ref[half:, :half] = -exact_dot(inverse, exact_dot(below_ref[...], top_ref[...], plain), plain)


def head_top(head):
    half = head.shape[0] // 2
    return pl.pallas_call(
        top_kernel, out_shape=[jax.ShapeDtypeStruct((half, half), jnp.float32)] * 3, name="head_top"
    )(head)


def head_low(top, below, rest):
    size = 2 * top.shape[0]
    return pl.pallas_call(
        low_kernel, out_shape=jax.ShapeDtypeStruct((size, size), jnp.float32), name="head_low"
    )(top, below, rest)


def on_device(features, signals, param_scale, geometry, electrons):
    par_size = lax.axis_size("par")
    walk_size = lax.axis_size("walk")
    walk_index = lax.axis_index("walk")
    par_index = lax.axis_index("par")
    per_device, slots_count, width = features.shape
    walkers = geometry.shape[0]
    groups = electrons.shape[0]
    row_block = per_device * par_size
    col_block = walkers // par_size
    plan = Plan(walk_size, par_size)

    anchor = (walk_index * par_size + par_index) * per_device
    own_geometry = lax.dynamic_slice_in_dim(geometry, anchor, per_device)
    own_matches = own_geometry[:, None] == jnp.arange(groups, dtype=jnp.int32)[None, :]
    own_electrons = jnp.sum(jnp.where(own_matches, electrons[None, :], 0), axis=1)
    live = (jnp.arange(slots_count, dtype=jnp.int32)[None, :] < own_electrons[:, None]).astype(jnp.float32)

    own = {"F": 0, "S": 0}
    for k, (axis, bit, kind) in enumerate(plan.dims):
        index = walk_index if axis == "walk" else par_index
        side = "F" if kind == "I" else "S"
        own[side] = own[side] + jnp.where((index & bit) != 0, 1 << plan.place[k], 0)
    flat = per_device * slots_count
    counts = (plan.blocks["F"], plan.blocks["S"])
    turned = turned_pieces(
        jnp.stack([own["F"], own["S"]]).astype(jnp.int32),
        live.reshape(1, flat),
        features.reshape(flat, width),
        signals.reshape(flat, width),
        counts,
    )
    names = [("F", 0, rb) for rb in range(counts[0])] + [("S", 0, rb) for rb in range(counts[1])]
    pieces = dict(zip(names, turned))
    ib, jb = width // plan.blocks["F"], width // plan.blocks["S"]
    parts = LANES // jb
    scaling = param_scale * (1.0 / math.sqrt(slots_count * width * width))
    scaling = lax.dynamic_slice(scaling, (own["F"] * ib, own["S"] * jb), (ib, jb))
    scaling = scaling.reshape(parts, ib // parts, jb).transpose(1, 0, 2).reshape(ib // parts, LANES)
    columns, names = exchange(plan, pieces, lambda f, s: jacobian(f, s, scaling, slots_count))
    place_at = []
    for src, core in [n for members in names for n in members]:
        walk_flip, par_flip = plan.flip(src)
        place_at.append((walk_index ^ (walk_flip | core)) * par_size + (par_index ^ par_flip))
    place_at = (jnp.stack(place_at) * per_device).astype(jnp.int32)

    matches = geometry[:, None] == jnp.arange(groups, dtype=jnp.int32)[None, :]
    hot = matches.astype(jnp.bfloat16)
    hot_t = (jnp.arange(groups, dtype=jnp.int32)[:, None] == geometry[None, :]).astype(jnp.bfloat16)
    counts = jnp.maximum(jnp.sum(matches.astype(jnp.float32), axis=0), 1.0)
    recip = (1.0 / counts)[:, None]

    chip_bits = walk_size.bit_length() - 2
    slots = 1 << chip_bits
    core, chip = walk_index & 1, walk_index >> 1
    row_at = jnp.stack([((chip ^ s) * 2 + core) * row_block for s in range(slots)]).astype(jnp.int32)
    col_at = jnp.stack([(par_index ^ p) * col_block for p in range(par_size)]).astype(jnp.int32)
    up = list(range(chip_bits))
    sweeps = (up, up[::-1])
    orders = tuple(
        tuple(sorted(range(slots), key=lambda s, o=o: [s >> b & 1 for b in o])) for o in sweeps
    )
    head_cols, far, near = gram_rows(
        columns, hot, hot_t, recip, row_at, col_at, place_at, row_block, col_block, orders
    )

    def after(values, *others):
        tied = lax.optimization_barrier(tuple(values) + others)
        return list(tied[: len(values)])

    def plane_step(pair, step):
        mid = pair[0].shape[0] // 2
        return [permute(pair[h][mid:], "walk", walk_size, 2 << sweeps[h][step]) for h in range(2)]

    def plane_add(pair, moved):
        return [pair[h][: pair[h].shape[0] // 2] + moved[h] for h in range(2)]

    far, near = list(far), list(near)
    head_cols = plane_add(head_cols, plane_step(head_cols, 0))
    tied = after([*head_cols, *far, *near])
    head_cols, far, near = tied[:2], tied[2:4], tied[4:]
    far_moved = plane_step(far, 0)
    for step in range(1, chip_bits):
        head_cols = plane_add(head_cols, plane_step(head_cols, step))
    rows_mine = jnp.concatenate(head_cols, axis=1)
    bit = par_size // 2
    rows_mine = rows_mine + permute(rows_mine, "par", par_size, bit)
    far = plane_add(far, far_moved)
    tied = after([rows_mine, *far, *near])
    rows_mine, far, near = tied[0], tied[1:3], tied[3:]
    near_moved = plane_step(near, 0)
    for step in range(1, chip_bits):
        far_moved = plane_step(far, step)
        if step < chip_bits - 1:
            far = plane_add(far, far_moved)
    bit //= 2
    while bit:
        rows_mine = rows_mine + permute(rows_mine, "par", par_size, bit)
        bit //= 2

    chips = walk_size // 2
    assert chips == par_size and col_block == 2 * row_block and row_block < PB <= 2 * row_block
    landed = [rows_mine]
    for flip in range(1, chips):
        pairs = []
        for z in range(par_size):
            for holder in sorted({0, z}):
                for c in range(2):
                    pairs.append(((holder * 2 + c) * par_size + z, ((holder ^ flip) * 2 + c) * par_size + z))
        landed.append(lax.ppermute(rows_mine, ("walk", "par"), pairs))
    landed = jnp.stack(landed)
    both = jnp.stack(
        [lax.dynamic_index_in_dim(landed, n, 0, keepdims=False) for n in (chip, chip ^ par_index)]
    )
    far = plane_add(far, far_moved)
    both, far[0], far[1] = after([both, *far])
    far = [permute(part, "par", par_size, par_size // 2) for part in far]
    swapped = permute(both, "walk", walk_size, 1)
    near = plane_add(near, near_moved)
    swapped, near[0], near[1] = after([swapped, *near])
    for step in range(1, chip_bits):
        near_moved = plane_step(near, step)
        if step < chip_bits - 1:
            near = plane_add(near, near_moved)
    pair = [jnp.where(core == 0, both, swapped), jnp.where(core == 0, swapped, both)]
    head = jnp.concatenate([pair[0][0], pair[1][0]], axis=0)[:PB]
    col_rows = jnp.concatenate([pair[0][1], pair[1][1]], axis=0)

    def shift_at(first_row, count):
        ids = first_row + jnp.arange(count, dtype=jnp.int32)
        return SHIFT * (ids[:, None] == jnp.arange(PB, dtype=jnp.int32)[None, :]).astype(jnp.float32)

    first = head_top(head + shift_at(0, PB))
    near = plane_add(near, near_moved)
    tied = after([*first, *near])
    first, near = tied[:3], tied[3:]
    inverse = head_low(*first)
    near = [part + got for part, got in zip(near, far)]
    moved = permute(near[1], "par", par_size, par_size // 4)
    inverse, near[0], near[1] = after([inverse, *near])
    panels = outer_rows(
        jnp.concatenate(
            [
                rows_mine + shift_at(walk_index * row_block, row_block),
                col_rows + shift_at(par_index * col_block, col_block),
            ],
            axis=0,
        ),
        inverse,
    )
    own_panel, col_panel = panels[:row_block], panels[row_block:]
    update = outer_rows(own_panel, col_panel)
    gram = near[0] + moved
    bit = par_size // 8
    while bit:
        mid = gram.shape[1] // 2
        gram = gram[:, :mid] + permute(gram[:, mid:], "par", par_size, bit)
        bit //= 2
    row_ids = walk_index * row_block + jnp.arange(row_block, dtype=jnp.int32)
    col_ids = par_index * col_block + jnp.arange(col_block, dtype=jnp.int32)
    shifted = gram + SHIFT * (row_ids[:, None] == col_ids[None, :]).astype(jnp.float32)
    return (own_panel, shifted - update)


def solution(mesh):
    in_specs = (P(("walk", "par"), None, None), P(("walk", "par"), None, None), P(), P(), P())
    out_specs = (P("walk", None), P("walk", "par"))
    return jax.shard_map(
        on_device, mesh=mesh, in_specs=in_specs, out_specs=out_specs, check_vma=False
    )
```
